32 devices in a mesh: groups: 2 (over y), frames: 4 (over z), heads: 4 (over x, core).
Axes of the slice: x: 2, y: 2, z: 4, core: 2. Of those that a mesh axis runs over, the one named last changes fastest.
Arguments:
- tokens: bfloat16 [64, 128, 1024], P(('groups', 'frames')), parts along dimension 0, may hold values from -12 to 12
- w_qkv: bfloat16 [1024, 3, 1024], P(None, None, 'heads'), may hold values from -1 to 1
- w_out: bfloat16 [1024, 1024], P('heads'), may hold values from -2 to 2
- pair_slots: int32 [16, 2], P(('groups', 'frames')), parts along dimension 0, may hold values from -1 to 31, as said below
Outputs:
- mixed: bfloat16 [64, 128, 1024], P(('groups', 'frames'), 'heads'), parts along dimension 0
The draws below stay inside these ranges and needn't reach their ends.
There are 2 independent parts, one for each index of `groups`. The reference program is written for one: setup_inputs(seed, part) draws one part's arguments, and reference() takes and returns one part's arrays. A program takes and returns all parts, laid end to end along the dimension named above; an argument that names none is the same for every part. Nothing has to cross between parts.
Inputs may be any that keep to these rules, and one draw needn't show every extreme that they name: `pair_slots`: rows 2 * o to 2 * o + 1 are the pairs owned by device o of the frames axis, which holds frames 8 * o to 8 * o + 7. A row is two frame indices or -1 twice; in each owner's block the live rows come first, and one owner has all 2 rows live. In one owner's block no two entries of live rows belong to the same home device (frame index // 8), so a frame appears there at most once.
All inputs are finite; a program needn't handle non-finite values.
Results may differ from the reference program's by a relative error of at most 0.0081.
Values may be sent and summed in bfloat16 or wider, within the bound.
A program may use at most 64 MiB of HBM per device.

```python
import jax
import jax.numpy as jnp
from jax import lax

D = 1024
HD = 64
TOK_FR = 128
FR_DEV = 8
FRAMES = 32
CAP = 2
SLOTS = 8


def draw_tokens(key, part):
    base = jax.random.normal(jax.random.fold_in(key, 1), (FRAMES, TOK_FR, D), jnp.float32)
    return jnp.clip(base, -12.0, 12.0).astype(jnp.bfloat16)


def draw_w_qkv(key, part):
    scale = D ** (-0.5)
    query_part = jax.random.normal(jax.random.fold_in(key, 1), (D, D), jnp.float32) * (1.2 * scale)
    key_part = jax.random.normal(jax.random.fold_in(key, 2), (D, D), jnp.float32) * (1.2 * scale)
    value_part = jax.random.normal(jax.random.fold_in(key, 3), (D, D), jnp.float32) * scale
    stacked = jnp.stack([query_part, key_part, value_part], axis=1)
    return jnp.clip(stacked, -1.0, 1.0).astype(jnp.bfloat16)


def draw_pair_slots(key, part):
    owner_count = SLOTS // CAP

    def one_owner(owner):
        sub_key = jax.random.fold_in(key, owner)
        order = jax.random.permutation(jax.random.fold_in(sub_key, 1), owner_count)
        local = jax.random.randint(jax.random.fold_in(sub_key, 2), (2 * CAP,), 0, FR_DEV)
        chosen = order[:2 * CAP] * FR_DEV + local
        return chosen.reshape(CAP, 2)
    owners = jnp.arange(owner_count)
    listing = jax.vmap(one_owner)(owners)
    live_count = jax.random.randint(jax.random.fold_in(key, 3), (owner_count,), 1, CAP + 1)
    fullest = jax.random.randint(jax.random.fold_in(key, 4), (), 0, owner_count)
    live_count = jnp.where(owners == fullest, CAP, live_count)
    is_live = jnp.arange(CAP)[None, :] < live_count[:, None]
    listing = jnp.where(is_live[:, :, None], listing, -1)
    return listing.reshape(owner_count * CAP, 2).astype(jnp.int32)


def shard_levels(key, shape, cuts, least, high):
    level = 1.0
    for dim, parts in cuts:
        heights = jax.random.uniform(jax.random.fold_in(jax.random.fold_in(key, 6), dim), (parts,), jnp.float32, least / len(cuts), high / len(cuts))
        level = level * jnp.repeat(jnp.exp(heights), shape[dim] // parts).reshape((-1,) + (1,) * (len(shape) - 1 - dim))
    return level


def centred(own_key, shape, width, reach, split=(), dtype=jnp.bfloat16):
    array = jax.random.normal(own_key, shape, jnp.float32) * width
    if len(split) > 0:
        array = shard_levels(own_key, shape, split, -0.22, 0.18) * array
    return jnp.clip(array, min=-reach, max=reach).astype(dtype)


def setup_inputs(seed: int = 0, part: int = 0) -> dict:
    streams_of = jax.random.split(jax.random.key(seed), 5)
    own_keys = jax.random.split(jax.random.fold_in(streams_of[4], part), 5)
    tokens = draw_tokens(jax.random.fold_in(jax.random.fold_in(streams_of[4], part), 71), part)
    w_qkv = draw_w_qkv(jax.random.fold_in(streams_of[4], 71), part)
    w_out = centred(streams_of[2], (D, D), 8 ** -0.5, 2.0, ((0, 4),))
    pair_slots = draw_pair_slots(jax.random.fold_in(jax.random.fold_in(streams_of[4], part), 71), part)
    return dict(tokens=tokens, w_qkv=w_qkv, w_out=w_out, pair_slots=pair_slots)


def attend(queries, key_rows, values):
    length, breadth = queries.shape
    head_count = breadth // HD
    query_heads = queries.reshape(length, head_count, HD).astype(jnp.float32)
    key_heads = key_rows.reshape(key_rows.shape[0], head_count, HD).astype(jnp.float32)
    value_heads = values.reshape(values.shape[0], head_count, HD).astype(jnp.float32)
    scores = jnp.einsum("qhd,khd->hqk", query_heads, key_heads) * (HD ** -0.5)
    row_peak = jnp.max(scores, axis=2)
    lifted = jnp.exp(scores - row_peak[:, :, None])
    row_total = jnp.sum(lifted, axis=2)
    rounded = lifted.astype(jnp.bfloat16).astype(jnp.float32)
    weighted = jnp.einsum("hqk,khd->qhd", rounded, value_heads)
    normalized = weighted / jnp.transpose(row_total)[:, :, None]
    return normalized.reshape(length, breadth), row_peak + jnp.log(row_total)


def merge_into(state, frame, new_out, new_lse):
    acc_out, acc_lse = state
    old_out = acc_out[frame]
    old_lse = acc_lse[frame]
    ceiling = jnp.maximum(old_lse, new_lse)
    old_weight = jnp.exp(old_lse - ceiling)
    new_weight = jnp.exp(new_lse - ceiling)
    weight_total = old_weight + new_weight
    length, breadth = old_out.shape
    head_count = old_lse.shape[0]
    old_split = old_out.reshape(length, head_count, HD)
    new_split = new_out.reshape(length, head_count, HD)
    combined = (jnp.transpose(old_weight)[:, :, None] * old_split + jnp.transpose(new_weight)[:, :, None] * new_split) / jnp.transpose(weight_total)[:, :, None]
    acc_out = acc_out.at[frame].set(combined.reshape(length, breadth))
    acc_lse = acc_lse.at[frame].set(ceiling + jnp.log(weight_total))
    return acc_out, acc_lse


def reference(tokens, w_qkv, w_out, pair_slots):
    frames_all, length, width_model = tokens.shape
    packed = jnp.dot(tokens.reshape(frames_all * length, width_model), w_qkv.reshape(width_model, 3 * width_model), preferred_element_type=jnp.float32).astype(jnp.bfloat16)
    packed = packed.reshape(frames_all, length, 3 * width_model)
    queries = packed[:, :, :width_model]
    key_rows = packed[:, :, width_model:2 * width_model]
    values = packed[:, :, 2 * width_model:]

    def self_part(trio):
        return attend(trio[0], trio[1], trio[2])

    self_out, self_lse = lax.map(self_part, (queries, key_rows, values))

    def visit(state, slot_pair):
        first_frame = jnp.maximum(slot_pair[0], 0).astype(jnp.int32)
        second_frame = jnp.maximum(slot_pair[1], 0).astype(jnp.int32)

        def update(inner):
            out_first, lse_first = attend(queries[first_frame], key_rows[second_frame], values[second_frame])
            out_second, lse_second = attend(queries[second_frame], key_rows[first_frame], values[first_frame])
            inner = merge_into(inner, first_frame, out_first, lse_first)
            return merge_into(inner, second_frame, out_second, lse_second)

        def keep(inner):
            return inner

        return lax.cond(slot_pair[0] >= 0, update, keep, state), None

    final_state, _ = lax.scan(visit, (self_out, self_lse), pair_slots)
    merged = final_state[0].astype(jnp.bfloat16)
    mixed = jnp.dot(merged.reshape(frames_all * length, width_model), w_out, preferred_element_type=jnp.float32)
    return mixed.astype(jnp.bfloat16).reshape(frames_all, length, width_model)
```

```python
import functools

import jax
import jax.numpy as jnp
from jax import lax
from jax.experimental import pallas as pl
from jax.experimental.pallas import tpu as pltpu
from jax.sharding import PartitionSpec as P

HD = 64
MESH = pl.DeviceIdType.MESH


def repeat(count, body):
    if count <= 8:
        for step in range(count):
            body(step)
    else:

        def step_body(step, carry):
            body(step)
            return carry

        lax.fori_loop(0, count, step_body, 0)


def kernel(
    devices, parts, cap, groups_out,
    pairs_ref, x_hbm, w_hbm, wo_hbm, out_ref,
    x_ref, w_ref, slots, listing, listing_s, info, q_ref, k_ref, v_ref,
    send1, recv1, send2, xs,
    so, sm, sl, top, po, pm, psum, msend, mrecv, wall,
    x_sem, w_sem, wo_sem, list_send, list_recv, local_sem,
    h1_send, h1_recv, h2_send, h2_recv, g_send, g_recv,
    w_send, w_recv, m_send, m_recv,
):
    me = lax.axis_index("frames")
    part = lax.axis_index("heads")
    frames_here, length, breadth = q_ref.shape
    width = x_ref.shape[2]
    heads = breadth // HD
    share = length // parts
    per = 256 // length
    chunks = frames_here // per
    group = frames_here // groups_out

    def frame_peer(step):
        return lax.rem(me + step + 1, devices)

    def head_peer(step):
        return lax.rem(part + step + 1, parts)

    barrier = pltpu.get_barrier_semaphore()

    def greet_frames(step):
        pl.semaphore_signal(
            barrier, inc=1, device_id={"frames": frame_peer(step)}, device_id_type=MESH
        )

    def greet_heads(step):
        pl.semaphore_signal(
            barrier, inc=1, device_id={"heads": head_peer(step)}, device_id_type=MESH
        )

    repeat(devices - 1, greet_frames)
    repeat(parts - 1, greet_heads)

    def x_copy(i):
        rows = pl.ds(i * per, per)
        return pltpu.make_async_copy(x_hbm.at[rows], x_ref.at[rows], x_sem.at[i])

    def w_load(which):
        return pltpu.make_async_copy(w_hbm.at[which], w_ref.at[which], w_sem.at[which])

    wo_load = pltpu.make_async_copy(wo_hbm, wall.at[part], wo_sem)
    w_load(1).start()
    for i in range(chunks):
        x_copy(i).start()
    w_load(2).start()
    w_load(0).start()
    wo_load.start()

    slots[...] = jnp.zeros_like(slots)
    slots[: pairs_ref.shape[0], : pairs_ref.shape[1]] = pairs_ref[...]
    listing[me] = slots[...]

    def own_rows(block):
        return pl.ds(pl.multiple_of(block * share, share), share)

    def hop1(step):
        peer = frame_peer(step)
        return pltpu.make_async_remote_copy(
            send1.at[peer], recv1.at[me], h1_send.at[step], h1_recv.at[step],
            device_id={"frames": peer}, device_id_type=MESH,
        )

    def hop2(step):
        peer = frame_peer(step)
        return pltpu.make_async_remote_copy(
            send2.at[peer], xs.at[me, own_rows(part)], h2_send.at[step], h2_recv.at[step],
            device_id={"frames": peer}, device_id_type=MESH,
        )

    def list_copy(step):
        return pltpu.make_async_remote_copy(
            slots, listing.at[me], list_send.at[step], list_recv.at[step],
            device_id={"frames": frame_peer(step)}, device_id_type=MESH,
        )

    pairwise = parts == 4
    near = part + 1 - 2 * lax.rem(part, 2)
    across = lax.rem(part + 2, parts)

    def w_copy(step):
        if pairwise:
            block = across if step == 2 else part
            peer = across if step == 0 else near
        else:
            block = part
            peer = head_peer(step)
        return pltpu.make_async_remote_copy(
            wall.at[block], wall.at[block], w_send.at[step], w_recv.at[step],
            device_id={"heads": peer}, device_id_type=MESH,
        )

    def slot_of(k):
        return lax.rem(me + devices - k, devices)

    def g_copy(k, step):
        block = part
        peer = head_peer(step)
        piece = xs.at[slot_of(k), own_rows(block)]
        return pltpu.make_async_remote_copy(
            piece, piece, g_send.at[k, step], g_recv.at[k, step],
            device_id={"heads": peer}, device_id_type=MESH,
        )

    def spread(k):
        for step in range(parts - 1):
            g_copy(k, step).start()

    def collect(k):
        for step in range(parts - 1):
            g_copy(k, step).wait()

    def m_copy(g, step):
        peer = head_peer(step)
        return pltpu.make_async_remote_copy(
            msend.at[g, peer], mrecv.at[g, part], m_send.at[g, step], m_recv.at[g, step],
            device_id={"heads": peer}, device_id_type=MESH,
        )

    def project(which, target, first):
        w_load(which).wait()

        def body(i, carry):
            if first:
                x_copy(i).wait()
            rows = x_ref[pl.ds(i * per, per)].reshape(per * length, width)
            made = jnp.dot(rows, w_ref[which], preferred_element_type=jnp.float32)
            target[pl.ds(i * per, per)] = made.astype(jnp.bfloat16).reshape(per, length, breadth)
            return carry

        lax.fori_loop(0, chunks, body, 0)

    project(1, k_ref, True)
    pl.semaphore_wait(barrier, devices + parts - 2)
    repeat(devices - 1, lambda s: list_copy(s).start())
    wo_load.wait()
    for s in range(2 if pairwise else parts - 1):
        w_copy(s).start()
    repeat(devices - 1, lambda s: list_copy(s).wait())
    to_scalar = pltpu.make_async_copy(listing, listing_s, local_sem)
    to_scalar.start()
    to_scalar.wait()

    def gather(owner):
        low = me * frames_here
        frame = jnp.int32(0)
        live = jnp.int32(-1)
        for entry in range(2 * cap):
            value = listing_s[owner, entry // 2, entry % 2]
            hit = (value >= low) & (value < low + frames_here)
            frame = jnp.where(hit, value - low, frame)
            live = jnp.where(hit, value - low, live)
        info[0, owner] = frame
        info[1, owner] = live
        send1[owner] = x_ref[frame, own_rows(part)]

    repeat(devices, gather)
    repeat(devices - 1, lambda s: hop1(s).start())
    recv1[me] = send1[me]

    project(2, v_ref, False)
    lane_head = lax.broadcasted_iota(jnp.int32, (length, breadth), 1) // HD

    def pick(array):
        shown = jnp.broadcast_to(array[:length], (length, breadth))
        for h in range(1, heads):
            shown = jnp.where(
                lane_head == h,
                jnp.broadcast_to(array[h * length : (h + 1) * length], (length, breadth)),
                shown,
            )
        return shown

    def lift(queries, key_rows):
        stacked = jnp.concatenate(
            [jnp.where(lane_head == h, queries, jnp.zeros_like(queries)) for h in range(heads)],
            axis=0,
        )
        scores = lax.dot_general(
            stacked, key_rows, (((1,), (1,)), ((), ())), preferred_element_type=jnp.float32
        ) * (HD ** -0.5)
        peak = jnp.max(scores, axis=1, keepdims=True)
        lifted = jnp.exp(scores - peak)
        total = jnp.sum(lifted, axis=1, keepdims=True)
        return lifted.astype(jnp.bfloat16), pick(peak), pick(total)

    def self_body(f, carry):
        e, m, l = lift(q_ref[f], k_ref[f])
        so[f] = pick(jnp.dot(e, v_ref[f], preferred_element_type=jnp.float32))
        sm[f] = m
        sl[f] = l
        return carry

    def relay(dest):
        low = dest * frames_here
        partner = me
        for row in range(cap):
            a = listing_s[me, row, 0]
            b = listing_s[me, row, 1]
            hit_a = (a >= low) & (a < low + frames_here)
            hit_b = (b >= low) & (b < low + frames_here)
            partner = jnp.where(hit_a, lax.div(b, jnp.int32(frames_here)), partner)
            partner = jnp.where(hit_b, lax.div(a, jnp.int32(frames_here)), partner)
        send2[dest] = recv1[partner]

    repeat(devices - 1, lambda s: hop1(s).wait())
    repeat(devices, relay)
    repeat(devices - 1, lambda s: hop2(s).start())
    xs[me, own_rows(part)] = send2[me]
    spread(0)
    project(0, q_ref, False)

    def pair_attend(k):
        owner = slot_of(k)
        rows = xs[owner]
        keys = jnp.dot(rows, w_ref[1], preferred_element_type=jnp.float32).astype(jnp.bfloat16)
        values = jnp.dot(rows, w_ref[2], preferred_element_type=jnp.float32).astype(jnp.bfloat16)
        e, m, l = lift(q_ref[info[0, owner]], keys)
        po[owner] = pick(jnp.dot(e, values, preferred_element_type=jnp.float32))
        pm[owner] = m
        psum[owner] = l

    def arrived(step):
        hop2(step).wait()
        spread(step + 1)

    def finish(k):
        collect(k)
        pair_attend(k)

    repeat(devices - 1, arrived)
    lax.fori_loop(0, frames_here, self_body, 0)

    if pairwise:
        w_copy(0).wait()
        w_copy(2).start()
    finish(0)
    repeat(devices - 1, lambda s: finish(s + 1))


    def peak_body(f, carry):
        def raise_peak(owner, peak):
            return jnp.maximum(peak, jnp.where(info[1, owner] == f, pm[owner], -jnp.inf))

        peak = lax.fori_loop(0, devices, raise_peak, sm[f], unroll=devices <= 8)
        top[f] = peak
        weight = jnp.exp(sm[f] - peak)
        sm[f] = weight
        sl[f] = weight * sl[f]
        return carry

    lax.fori_loop(0, frames_here, peak_body, 0)

    def pair_weight(owner):
        live = info[1, owner] >= 0
        weight = jnp.where(live, jnp.exp(pm[owner] - top[info[0, owner]]), 0.0)
        weight = jnp.where(live, weight, 0.0)
        pm[owner] = weight
        psum[owner] = weight * psum[owner]

    repeat(devices, pair_weight)

    def den_body(f, carry):
        def add(owner, den):
            return den + jnp.where(info[1, owner] == f, psum[owner], 0.0)

        den = lax.fori_loop(0, devices, add, sl[f], unroll=devices <= 8)
        inverse = 1.0 / den
        top[f] = inverse
        so[f] = so[f] * (sm[f] * inverse)
        return carry

    lax.fori_loop(0, frames_here, den_body, 0)

    def pair_scale(owner):
        po[owner] = po[owner] * (pm[owner] * top[info[0, owner]])

    repeat(devices, pair_scale)

    for g in range(groups_out):

        def merge_body(i, carry):
            f = g * group + i

            def add(owner, state):
                return state + jnp.where(info[1, owner] == f, po[owner], 0.0)

            merged = lax.fori_loop(0, devices, add, so[f], unroll=devices <= 8)
            merged = merged.astype(jnp.bfloat16)
            for h in range(parts):
                msend[g, h, i] = merged[h * share : (h + 1) * share]
            return carry

        lax.fori_loop(0, group, merge_body, 0)
        for s in range(parts - 1):
            m_copy(g, s).start()
        mrecv[g, part] = msend[g, part]

    for s in range(1 if pairwise else 0, parts - 1):
        w_copy(s).wait()
    for g in range(groups_out):
        for s in range(parts - 1):
            m_copy(g, s).wait()
        total = jnp.zeros((group * share, width), jnp.float32)
        for h in range(parts):
            total = total + jnp.dot(
                mrecv[g, h].reshape(group * share, breadth),
                wall[h],
                preferred_element_type=jnp.float32,
            )
        out_ref[pl.ds(g * group, group)] = total.astype(jnp.bfloat16).reshape(
            group, share, width
        )


def local(tokens, w_qkv, w_out, pair_slots):
    frames_here, length, width = tokens.shape
    breadth = w_qkv.shape[2]
    devices = lax.axis_size("frames")
    parts = lax.axis_size("heads")
    cap = pair_slots.shape[0]
    share = length // parts
    rows = -(-cap // 8) * 8
    groups_out = 2
    group = frames_here // groups_out
    bf, f32 = jnp.bfloat16, jnp.float32
    vm = pl.BlockSpec(memory_space=pltpu.VMEM)
    hbm = pl.BlockSpec(memory_space=pl.ANY)
    dma = pltpu.SemaphoreType.DMA
    frame_bf = pltpu.VMEM((frames_here, length, breadth), bf)
    frame_f = pltpu.VMEM((frames_here, length, breadth), f32)
    slot_bf = pltpu.VMEM((devices, share, width), bf)
    slot_f = pltpu.VMEM((devices, length, breadth), f32)
    return pl.pallas_call(
        functools.partial(kernel, devices, parts, cap, groups_out),
        out_shape=pltpu.VMEM((frames_here, share, width), bf),
        in_specs=[vm, hbm, hbm, hbm],
        out_specs=vm,
        scratch_shapes=[
            pltpu.VMEM((frames_here, length, width), bf),
            pltpu.VMEM((3, width, breadth), bf),
            pltpu.VMEM((rows, 128), jnp.int32),
            pltpu.VMEM((devices, rows, 128), jnp.int32),
            pltpu.SMEM((devices, rows, 128), jnp.int32),
            pltpu.SMEM((2, devices), jnp.int32),
        ]
        + [frame_bf] * 3
        + [slot_bf] * 3
        + [pltpu.VMEM((devices, length, width), bf)]
        + [frame_f] * 4
        + [slot_f] * 3
        + [
            pltpu.VMEM((groups_out, parts, group, share, breadth), bf),
            pltpu.VMEM((groups_out, parts, group, share, breadth), bf),
            pltpu.VMEM((parts, breadth, width), bf),
            dma((frames_here * length // 256,)),
            dma((3,)),
            dma,
            dma((devices - 1,)),
            dma((devices - 1,)),
            dma,
        ]
        + [dma((devices - 1,))] * 4
        + [dma((devices, parts - 1))] * 2
        + [dma((parts - 1,))] * 2
        + [dma((groups_out, parts - 1))] * 2,
        compiler_params=pltpu.CompilerParams(
            collective_id=0, has_side_effects=True, vmem_limit_bytes=60 * 1024 * 1024
        ),
    )(
        pair_slots,
        tokens,
        jnp.transpose(w_qkv, (1, 0, 2)),
        w_out,
    )


def solution(mesh):
    placed = (
        P(("groups", "frames"), None, None),
        P(None, None, "heads"),
        P("heads", None),
        P(("groups", "frames"), None),
    )
    return jax.shard_map(
        local,
        mesh=mesh,
        in_specs=placed,
        out_specs=P(("groups", "frames"), "heads", None),
        check_vma=False,
    )
```

```python
import functools

import jax
import jax.numpy as jnp
from jax import lax
from jax.experimental import pallas as pl
from jax.experimental.pallas import tpu as pltpu
from jax.sharding import PartitionSpec as P

HD = 64
MESH = pl.DeviceIdType.MESH


def repeat(count, body):
    if count <= 8:
        for step in range(count):
            body(step)
    else:

        def step_body(step, carry):
            body(step)
            return carry

        lax.fori_loop(0, count, step_body, 0)


def kernel(
    devices, parts, groups, cap,
    pairs_ref, x_hbm, w_hbm, wo_hbm, out_ref,
    info, x_ref, w_ref, wall, q_ref, k_ref, v_ref,
    idx_send, idx_recv, xsend, xs, qs, ks, vs,
    self_send, self_recv, self_lse, self_lse_recv,
    pair_send, pair_recv, pair_lse, pair_lse_recv,
    slot_weights, scaled, merged,
    x_sem, w_sem, wo_sem, i_send, i_recv, h_send, h_recv, g_send, g_recv,
    m_send, m_recv, ml_send, ml_recv, p_send, p_recv, pl_send, pl_recv, o_send, o_recv,
):
    me = lax.axis_index("frames")
    part = lax.axis_index("heads")
    group = lax.axis_index("groups")
    frames_here, length, breadth = q_ref.shape
    width = x_ref.shape[2]
    heads = breadth // HD
    share = length // parts
    lanes = heads * share
    per = 256 // length
    chunks = frames_here // per
    half = breadth // 2
    small = devices <= 8

    def peer(step):
        if devices == 4:
            low = lax.rem(me, 2)
            high = lax.div(me, 2)
            return (
                2 * high + 1 - low,
                2 * (1 - high) + low,
                3 - me,
            )[step]
        return lax.rem(me + step + 1, devices)

    def source(step):
        if devices == 4:
            return peer(step)
        return lax.rem(me + devices - step - 1, devices)

    def head_peer(step):
        return lax.rem(part + step, parts)

    mate = part + 1 - 2 * lax.rem(part, 2)
    across = lax.rem(part + 2, parts)

    def own_rows(block):
        return pl.ds(pl.multiple_of(block * share, share), share)

    barrier = pltpu.get_barrier_semaphore()

    def greet(step):
        for j in range(parts):
            pl.semaphore_signal(
                barrier, inc=1,
                device_id={"frames": peer(step), "heads": head_peer(j)},
                device_id_type=MESH,
            )

    repeat(devices - 1, greet)
    for j in range(1, parts):
        pl.semaphore_signal(
            barrier, inc=1, device_id={"heads": head_peer(j)}, device_id_type=MESH
        )
    for j in range(1, groups):
        pl.semaphore_signal(
            barrier, inc=1, device_id={"groups": lax.rem(group + j, groups)}, device_id_type=MESH
        )

    def x_copy(i):
        rows = pl.ds(i * per, per)
        return pltpu.make_async_copy(x_hbm.at[rows], x_ref.at[rows], x_sem.at[i])

    def w_load(which):
        return pltpu.make_async_copy(w_hbm.at[which], w_ref.at[which], w_sem.at[which])

    wo_load = pltpu.make_async_copy(wo_hbm, wall.at[part], wo_sem)
    w_load(1).start()
    for i in range(chunks):
        x_copy(i).start()
    wo_load.start()
    w_load(2).start()
    w_load(0).start()

    def look(home):
        low = home * frames_here
        frame = jnp.int32(-1)
        partner = jnp.int32(0) + me
        for row in range(cap):
            a = pairs_ref[row, 0]
            b = pairs_ref[row, 1]
            hit_a = (a >= low) & (a < low + frames_here)
            hit_b = (b >= low) & (b < low + frames_here)
            frame = jnp.where(hit_a, a - low, jnp.where(hit_b, b - low, frame))
            partner = jnp.where(
                hit_a, lax.div(b, jnp.int32(frames_here)),
                jnp.where(hit_b, lax.div(a, jnp.int32(frames_here)), partner),
            )
        info[0, home] = jnp.maximum(frame, 0)
        info[1, home] = partner
        idx_send[home] = jnp.full(idx_send.shape[1:], frame, jnp.int32)

    repeat(devices, look)
    idx_recv[me] = idx_send[me]

    def idx_copy(step):
        to = peer(step)
        return pltpu.make_async_remote_copy(
            idx_send.at[to], idx_recv.at[me], i_send.at[step], i_recv.at[step],
            device_id={"frames": to}, device_id_type=MESH,
        )

    def hop(step):
        to = peer(step)
        return pltpu.make_async_remote_copy(
            xsend.at[to], xs.at[me, own_rows(part)], h_send.at[step], h_recv.at[step],
            device_id={"frames": to}, device_id_type=MESH,
        )

    def g_copy(step, kind):
        rows = own_rows(across if kind == 2 else part)
        piece = xs.at[source(step), rows]
        return pltpu.make_async_remote_copy(
            piece, piece, g_send.at[step, kind], g_recv.at[step, kind],
            device_id={"heads": across if kind == 1 else mate}, device_id_type=MESH,
        )

    first_half = pl.ds(pl.multiple_of(group * half, half), half)
    second_half = pl.ds(pl.multiple_of((1 - group) * half, half), half)

    def w_copy(kind):
        piece = (
            wall.at[part],
            wall.at[part, first_half],
            wall.at[across, first_half],
            wall.at[across, first_half],
            wall.at[across, second_half],
        )[kind]
        target = (
            {"heads": mate},
            {"heads": across},
            {"groups": 1 - group},
            {"heads": mate},
            {"heads": mate},
        )[kind]
        return pltpu.make_async_remote_copy(
            piece, piece, o_send.at[kind], o_recv.at[kind],
            device_id=target, device_id_type=MESH,
        )

    def m_copy(step):
        to = head_peer(step)
        return pltpu.make_async_remote_copy(
            self_send.at[to], self_recv.at[part], m_send.at[step - 1], m_recv.at[step - 1],
            device_id={"heads": to}, device_id_type=MESH,
        )

    def ml_copy(step):
        to = head_peer(step)
        return pltpu.make_async_remote_copy(
            self_lse.at[to], self_lse_recv.at[part], ml_send.at[step - 1], ml_recv.at[step - 1],
            device_id={"heads": to}, device_id_type=MESH,
        )

    def pair_copies(step, j):
        own = isinstance(step, int) and step == devices - 1
        home = me if own else peer(step)
        to = head_peer(j)
        where = {"heads": to} if own else {"frames": home, "heads": to}
        return (
            pltpu.make_async_remote_copy(
                pair_send.at[home, to], pair_recv.at[me, part],
                p_send.at[step, j], p_recv.at[step, j],
                device_id=where, device_id_type=MESH,
            ),
            pltpu.make_async_remote_copy(
                pair_lse.at[home, to], pair_lse_recv.at[me, part],
                pl_send.at[step, j], pl_recv.at[step, j],
                device_id=where, device_id_type=MESH,
            ),
        )

    pl.semaphore_wait(barrier, devices * parts - 1 + groups - 1)
    repeat(devices - 1, lambda s: idx_copy(s).start())
    wo_load.wait()
    w_copy(1).start()
    w_copy(0).start()

    def project(which, target, first):
        w_load(which).wait()

        def body(i, carry):
            if first:
                x_copy(i).wait()
            rows = x_ref[pl.ds(i * per, per)].reshape(per * length, width)
            made = jnp.dot(rows, w_ref[which], preferred_element_type=jnp.float32)
            if which == 0:
                made = made * (HD ** -0.5)
            target[pl.ds(i * per, per)] = made.astype(jnp.bfloat16).reshape(per, length, breadth)
            return carry

        lax.fori_loop(0, chunks, body, 0)

    project(1, k_ref, True)
    project(2, v_ref, False)
    project(0, q_ref, False)

    def select(step):
        idx_copy(step).wait_recv()
        asked = idx_recv[source(step)]
        total = None
        for f in range(frames_here):
            unit = jnp.where(asked == f, 1.0, 0.0)
            unit = jnp.concatenate([unit, unit], axis=0).astype(jnp.bfloat16)
            unit = jnp.concatenate([unit] * (width // unit.shape[1]), axis=1)
            unit = jnp.concatenate([unit] * (share // unit.shape[0]), axis=0)
            term = x_ref[f, own_rows(part)] * unit
            total = term if total is None else total + term
        xsend[source(step)] = total

    def select_send(step):
        select(step)
        if devices == 4:
            hop(step).start()

    repeat(devices - 1, select_send)
    if devices != 4:
        repeat(devices - 1, lambda s: hop(s).start())

    lane_head = lax.broadcasted_iota(jnp.int32, (share, breadth), 1) // HD

    def attend(queries, key_rows, values):
        nothing = jnp.zeros((share, breadth), queries.dtype)
        stacked = jnp.concatenate(
            [
                jnp.where(lane_head == h, queries[p * share : (p + 1) * share], nothing)
                for p in range(parts)
                for h in range(heads)
            ],
            axis=0,
        )
        scores = lax.dot_general(
            key_rows, stacked, (((1,), (1,)), ((), ())), preferred_element_type=jnp.float32
        )
        peak = jnp.max(scores, axis=0, keepdims=True)
        lifted = jnp.exp(scores - peak)
        total = jnp.sum(lifted, axis=0, keepdims=True)
        shares = (lifted * (1.0 / total)).astype(jnp.bfloat16)
        lse = peak + jnp.log(total)
        wide = lax.dot_general(
            shares, values, (((0,), (0,)), ((), ())), preferred_element_type=jnp.float32
        )
        outs = []
        for p in range(parts):
            rows = wide[p * lanes : (p + 1) * lanes]
            shown = rows[:share]
            for h in range(1, heads):
                shown = jnp.where(lane_head == h, rows[h * share : (h + 1) * share], shown)
            outs.append(shown.astype(jnp.bfloat16))
        return outs, [lse[:, p * lanes : (p + 1) * lanes] for p in range(parts)]

    def self_body(f, carry):
        outs, lses = attend(q_ref[f], k_ref[f], v_ref[f])
        for p in range(parts):
            self_send[p, f] = outs[p]
            self_lse[p, pl.ds(f, 1)] = lses[p]
        return carry

    lax.fori_loop(0, frames_here, self_body, 0)

    own = info[0, me]
    qs[me] = q_ref[own]
    ks[me] = k_ref[own]
    vs[me] = v_ref[own]

    def arrive(step):
        hop(step).wait_recv()
        g_copy(step, 0).start()
        g_copy(step, 1).start()

    repeat(devices - 1, arrive)
    w_copy(1).wait_recv()
    w_copy(2).start()
    w_copy(3).start()

    def forward(step):
        g_copy(step, 1).wait_recv()
        g_copy(step, 2).start()

    repeat(devices - 1, forward)
    for j in range(1, parts):
        m_copy(j).start()
        ml_copy(j).start()
    self_recv[part] = self_send[part]
    self_lse_recv[part] = self_lse[part]

    def project_slot(step):
        g_copy(step, 0).wait_recv()
        g_copy(step, 2).wait_recv()
        home = source(step)
        rows = xs[home]
        for which, target in ((1, ks), (2, vs), (0, qs)):
            made = jnp.dot(rows, w_ref[which], preferred_element_type=jnp.float32)
            if which == 0:
                made = made * (HD ** -0.5)
            target[home] = made.astype(jnp.bfloat16)

    repeat(devices - 1, project_slot)

    def attend_slot(home):
        partner = info[1, home]
        outs, lses = attend(qs[home], ks[partner], vs[partner])
        for p in range(parts):
            pair_send[home, p] = outs[p]
            pair_lse[home, p] = lses[p]

    def slot_send(step):
        attend_slot(peer(step))
        for j in range(parts):
            for copy in pair_copies(step, j):
                copy.start()

    repeat(devices - 1, slot_send)
    attend_slot(me)
    for j in range(1, parts):
        for copy in pair_copies(devices - 1, j):
            copy.start()
    pair_recv[me, part] = pair_send[me, part]
    pair_lse_recv[me, part] = pair_lse[me, part]

    w_copy(2).wait_recv()
    w_copy(4).start()
    w_copy(0).wait_recv()
    for j in range(1, parts):
        m_copy(j).wait_recv()
        ml_copy(j).wait_recv()
    w_copy(3).wait_recv()
    w_copy(4).wait_recv()

    def pairs_in(step):
        for j in range(parts):
            for copy in pair_copies(step, j):
                copy.wait_recv()

    for j in range(1, parts):
        for copy in pair_copies(devices - 1, j):
            copy.wait_recv()
    repeat(devices - 1, pairs_in)

    row_frame = lax.broadcasted_iota(jnp.int32, (frames_here, lanes), 0)
    tables = []
    for g in range(parts):
        own_lse = self_lse_recv[g]

        def lifted_lse(owner, g=g):
            row = jnp.broadcast_to(pair_lse_recv[owner, g], (frames_here, lanes))
            return jnp.where(idx_recv[owner] == row_frame, row, -jnp.inf)

        peak = lax.fori_loop(
            0, devices, lambda o, p: jnp.maximum(p, lifted_lse(o)), own_lse, unroll=small
        )
        own_weight = jnp.exp(own_lse - peak)
        den = lax.fori_loop(
            0, devices, lambda o, d: d + jnp.exp(lifted_lse(o) - peak), own_weight, unroll=small
        )
        inverse = 1.0 / den
        tables.append(own_weight * inverse)

        def slot_weight(owner, g=g, peak=peak, inverse=inverse):
            weight = jnp.exp(lifted_lse(owner) - peak) * inverse
            slot_weights[owner, pl.ds(g, 1)] = jnp.sum(weight, axis=0, keepdims=True)

        repeat(devices, slot_weight)

    low_lane = lax.broadcasted_iota(jnp.int32, (share, 2 * HD), 1) < HD

    def spread(columns, c):
        picked = [
            jnp.broadcast_to(columns[h * share : (h + 1) * share, c : c + 1], (share, 2 * HD))
            for h in range(heads)
        ]
        return jnp.concatenate(
            [jnp.where(low_lane, picked[h], picked[h + 1]) for h in range(0, heads, 2)], axis=1
        )

    def scale_slot(owner):
        columns = jnp.transpose(slot_weights[owner])
        for g in range(parts):
            scaled[owner, :, g * breadth : (g + 1) * breadth] = (
                pair_recv[owner, g].astype(jnp.float32) * spread(columns, g)
            )

    repeat(devices, scale_slot)

    own_columns = jnp.transpose(jnp.concatenate(tables, axis=0))
    for f in range(frames_here):
        for g in range(parts):
            state = self_recv[g, f].astype(jnp.float32) * spread(own_columns, g * frames_here + f)

            def add(owner, state, g=g, f=f):
                hit = idx_recv[owner] == f
                hit = jnp.concatenate([hit] * (share // hit.shape[0]), axis=0)
                hit = jnp.concatenate([hit] * (breadth // hit.shape[1]), axis=1)
                return state + jnp.where(hit, scaled[owner, :, g * breadth : (g + 1) * breadth], 0.0)

            state = lax.fori_loop(0, devices, add, state, unroll=small)
            merged[f * share : (f + 1) * share, g * breadth : (g + 1) * breadth] = state.astype(
                jnp.bfloat16
            )

    for n in range(0, width, 256):
        total = None
        for g in range(parts):
            term = jnp.dot(
                merged[:, g * breadth : (g + 1) * breadth], wall[g, :, n : n + 256],
                preferred_element_type=jnp.float32,
            )
            total = term if total is None else total + term
        out_ref[:, :, n : n + 256] = total.astype(jnp.bfloat16).reshape(frames_here, share, 256)

    repeat(devices - 1, lambda s: idx_copy(s).wait_send())
    repeat(devices - 1, lambda s: hop(s).wait_send())

    def sent(step):
        for kind in range(3):
            g_copy(step, kind).wait_send()
        for j in range(parts):
            for copy in pair_copies(step, j):
                copy.wait_send()

    repeat(devices - 1, sent)
    for j in range(1, parts):
        m_copy(j).wait_send()
        ml_copy(j).wait_send()
        for copy in pair_copies(devices - 1, j):
            copy.wait_send()
    for kind in range(5):
        w_copy(kind).wait_send()


def local(tokens, w_qkv, w_out, pair_slots):
    frames_here, length, width = tokens.shape
    breadth = w_qkv.shape[2]
    devices = lax.axis_size("frames")
    parts = lax.axis_size("heads")
    groups = lax.axis_size("groups")
    cap = pair_slots.shape[0]
    share = length // parts
    lanes = breadth // HD * share
    bf, f32 = jnp.bfloat16, jnp.float32
    smem = pl.BlockSpec(memory_space=pltpu.SMEM)
    vm = pl.BlockSpec(memory_space=pltpu.VMEM)
    hbm = pl.BlockSpec(memory_space=pl.ANY)
    dma = pltpu.SemaphoreType.DMA
    vmem = pltpu.VMEM
    return pl.pallas_call(
        functools.partial(kernel, devices, parts, groups, cap),
        out_shape=pltpu.VMEM((frames_here, share, width), bf),
        in_specs=[smem, hbm, hbm, hbm],
        out_specs=vm,
        scratch_shapes=[
            pltpu.SMEM((2, devices), jnp.int32),
            vmem((frames_here, length, width), bf),
            vmem((3, width, breadth), bf),
            vmem((parts, breadth, width), bf),
        ]
        + [vmem((frames_here, length, breadth), bf)] * 3
        + [vmem((devices, frames_here, lanes), jnp.int32)] * 2
        + [vmem((devices, share, width), bf), vmem((devices, length, width), bf)]
        + [vmem((devices, length, breadth), bf)] * 3
        + [vmem((parts, frames_here, share, breadth), bf)] * 2
        + [vmem((parts, frames_here, lanes), f32)] * 2
        + [vmem((devices, parts, share, breadth), bf)] * 2
        + [vmem((devices, parts, 1, lanes), f32)] * 2
        + [
            vmem((devices, parts, lanes), f32),
            vmem((devices, share, width), f32),
            vmem((frames_here * share, width), bf),
        ]
        + [dma((frames_here * length // 256,)), dma((3,)), dma]
        + [dma((devices - 1,))] * 4
        + [dma((devices - 1, 3))] * 2
        + [dma((parts - 1,))] * 4
        + [dma((devices, parts))] * 4
        + [dma((5,))] * 2,
        compiler_params=pltpu.CompilerParams(
            collective_id=0, has_side_effects=True, vmem_limit_bytes=60 * 1024 * 1024
        ),
    )(
        pair_slots,
        tokens,
        jnp.transpose(w_qkv, (1, 0, 2)),
        w_out,
    )


def solution(mesh):
    placed = (
        P(("groups", "frames"), None, None),
        P(None, None, "heads"),
        P("heads", None),
        P(("groups", "frames"), None),
    )
    return jax.shard_map(
        local,
        mesh=mesh,
        in_specs=placed,
        out_specs=P(("groups", "frames"), "heads", None),
        check_vma=False,
    )
```

```python
import functools

import jax
import jax.numpy as jnp
from jax import lax
from jax.experimental import pallas as pl
from jax.experimental.pallas import tpu as pltpu
from jax.sharding import PartitionSpec as P

HD = 64
MESH = pl.DeviceIdType.MESH


def repeat(count, body):
    if count <= 8:
        for step in range(count):
            body(step)
    else:

        def step_body(step, carry):
            body(step)
            return carry

        lax.fori_loop(0, count, step_body, 0)


def kernel(
    devices, parts, groups, cap,
    pairs_ref, x_hbm, w_hbm, wo_hbm, out_ref,
    info, x_ref, w_ref, wall, q_ref, k_ref, v_ref,
    idx_send, idx_recv, xsend, xs, qs, ks, vs,
    self_send, self_recv, self_lse, self_lse_recv,
    pair_send, pair_recv, pair_lse, pair_lse_recv,
    slot_weights, scaled, merged,
    x_sem, w_sem, wo_sem, i_send, i_recv, h_send, h_recv, g_send, g_recv,
    m_send, m_recv, ml_send, ml_recv, p_send, p_recv, pl_send, pl_recv, o_send, o_recv,
):
    me = lax.axis_index("frames")
    part = lax.axis_index("heads")
    group = lax.axis_index("groups")
    frames_here, length, breadth = q_ref.shape
    width = x_ref.shape[2]
    heads = breadth // HD
    share = length // parts
    lanes = heads * share
    per = 256 // length
    chunks = frames_here // per
    half = breadth // 2
    cuts = 2
    sub = share // cuts
    here = devices - 1
    small = devices <= 8

    def peer(step):
        if devices == 4:
            low = lax.rem(me, 2)
            high = lax.div(me, 2)
            return (
                2 * high + 1 - low,
                2 * (1 - high) + low,
                3 - me,
            )[step]
        return lax.rem(me + step + 1, devices)

    def source(step):
        if devices == 4:
            return peer(step)
        return lax.rem(me + devices - step - 1, devices)

    def slot_to(step):
        return step if devices == 4 else devices - 2 - step

    def slot_of(home):
        if devices == 4:
            low = jnp.abs(lax.rem(home, 2) - lax.rem(me, 2))
            high = jnp.abs(lax.div(home, 2) - lax.div(me, 2))
            return lax.rem(low + 2 * high + 3, 4)
        return lax.rem(me - home - 1 + 2 * devices, devices)

    order = (1, 2, 0) if devices == 4 else None

    def each_peer(body, order=order):
        if devices != 4:
            repeat(devices - 1, body)
        else:
            for step in order:
                body(step)

    def head_peer(step):
        return lax.rem(part + step, parts)

    mate = part + 1 - 2 * lax.rem(part, 2)
    across = lax.rem(part + 2, parts)

    def own_rows(block):
        return pl.ds(pl.multiple_of(block * sub, sub), sub)

    barrier = pltpu.get_barrier_semaphore()

    def greet(step):
        pl.semaphore_signal(
            barrier, inc=1, device_id={"frames": peer(step)}, device_id_type=MESH
        )

    repeat(devices - 1, greet)
    for j in range(1, parts):
        pl.semaphore_signal(
            barrier, inc=1, device_id={"heads": head_peer(j)}, device_id_type=MESH
        )
    for j in range(1, groups):
        pl.semaphore_signal(
            barrier, inc=1, device_id={"groups": lax.rem(group + j, groups)}, device_id_type=MESH
        )

    def x_copy(i):
        rows = pl.ds(i * per, per)
        return pltpu.make_async_copy(x_hbm.at[rows], x_ref.at[rows], x_sem.at[i])

    def w_load(which):
        return pltpu.make_async_copy(w_hbm.at[which], w_ref.at[which], w_sem.at[which])

    wo_load = pltpu.make_async_copy(wo_hbm, wall.at[part], wo_sem)
    w_load(1).start()
    for i in range(chunks):
        x_copy(i).start()
    wo_load.start()
    w_load(2).start()
    w_load(0).start()

    def look(slot):
        home = me if isinstance(slot, int) and slot == here else source(slot)
        low = home * frames_here
        frame = jnp.int32(-1)
        partner = jnp.int32(0) + me
        for row in range(cap):
            a = pairs_ref[row, 0]
            b = pairs_ref[row, 1]
            hit_a = (a >= low) & (a < low + frames_here)
            hit_b = (b >= low) & (b < low + frames_here)
            frame = jnp.where(hit_a, a - low, jnp.where(hit_b, b - low, frame))
            partner = jnp.where(
                hit_a, lax.div(b, jnp.int32(frames_here)),
                jnp.where(hit_b, lax.div(a, jnp.int32(frames_here)), partner),
            )
        info[0, slot] = jnp.maximum(frame, 0)
        info[1, slot] = slot_of(partner)
        idx_send[slot] = jnp.full(idx_send.shape[1:], frame, jnp.int32)

    repeat(devices - 1, look)
    look(here)
    idx_recv[here] = idx_send[here]

    def idx_copy(step):
        to = peer(step)
        return pltpu.make_async_remote_copy(
            idx_send.at[slot_to(step)], idx_recv.at[step], i_send.at[step], i_recv.at[step],
            device_id={"frames": to}, device_id_type=MESH,
        )

    def hop(step, cut):
        return pltpu.make_async_remote_copy(
            xsend.at[cut, step], xs.at[cut, step, own_rows(part)],
            h_send.at[cut, step], h_recv.at[cut, step],
            device_id={"frames": peer(step)}, device_id_type=MESH,
        )

    def g_copy(step, cut, kind):
        piece = xs.at[cut, step, own_rows(across if kind == 2 else part)]
        return pltpu.make_async_remote_copy(
            piece, piece, g_send.at[cut, step, kind], g_recv.at[cut, step, kind],
            device_id={"heads": across if kind == 1 else mate}, device_id_type=MESH,
        )

    first_half = pl.ds(pl.multiple_of(group * half, half), half)
    second_half = pl.ds(pl.multiple_of((1 - group) * half, half), half)

    def w_copy(kind):
        piece = (
            wall.at[part],
            wall.at[part, first_half],
            wall.at[across, first_half],
            wall.at[across, first_half],
            wall.at[across, second_half],
        )[kind]
        target = (
            {"heads": mate},
            {"heads": across},
            {"groups": 1 - group},
            {"heads": mate},
            {"heads": mate},
        )[kind]
        return pltpu.make_async_remote_copy(
            piece, piece, o_send.at[kind], o_recv.at[kind],
            device_id=target, device_id_type=MESH,
        )

    def m_copy(step, i):
        to = head_peer(step)
        frames = pl.ds(i * (frames_here // 2), frames_here // 2)
        return pltpu.make_async_remote_copy(
            self_send.at[to, frames], self_recv.at[part, frames],
            m_send.at[step - 1, i], m_recv.at[step - 1, i],
            device_id={"heads": to}, device_id_type=MESH,
        )

    def ml_copy(step):
        to = head_peer(step)
        return pltpu.make_async_remote_copy(
            self_lse.at[to], self_lse_recv.at[part], ml_send.at[step - 1], ml_recv.at[step - 1],
            device_id={"heads": to}, device_id_type=MESH,
        )

    def pair_copies(step, j):
        own = isinstance(step, int) and step == devices - 1
        slot = step if own else slot_to(step)
        to = head_peer(j)
        where = {"heads": to} if own else {"frames": peer(step), "heads": to}
        return (
            pltpu.make_async_remote_copy(
                pair_send.at[slot, to], pair_recv.at[step, part],
                p_send.at[step, j], p_recv.at[step, j],
                device_id=where, device_id_type=MESH,
            ),
            pltpu.make_async_remote_copy(
                pair_lse.at[slot, to], pair_lse_recv.at[step, part],
                pl_send.at[step, j], pl_recv.at[step, j],
                device_id=where, device_id_type=MESH,
            ),
        )

    pl.semaphore_wait(barrier, devices - 1 + parts - 1 + groups - 1)
    repeat(devices - 1, lambda s: idx_copy(s).start())
    wo_load.wait()
    w_copy(1).start()
    w_copy(0).start()

    def project(which, target, first):
        w_load(which).wait()

        def body(i, carry):
            if first:
                x_copy(i).wait()
            rows = x_ref[pl.ds(i * per, per)].reshape(per * length, width)
            made = jnp.dot(rows, w_ref[which], preferred_element_type=jnp.float32)
            if which == 0:
                made = made * (HD ** -0.5)
            target[pl.ds(i * per, per)] = made.astype(jnp.bfloat16).reshape(per, length, breadth)
            return carry

        lax.fori_loop(0, chunks, body, 0)

    project(1, k_ref, True)

    def select(step, cut):
        asked = idx_recv[slot_to(step)]
        rows = pl.ds(pl.multiple_of(part * share + cut * sub, sub), sub)
        total = None
        for f in range(frames_here):
            unit = jnp.where(asked == f, 1.0, 0.0)
            unit = jnp.concatenate([unit, unit], axis=0).astype(jnp.bfloat16)
            unit = jnp.concatenate([unit] * (width // unit.shape[1]), axis=1)
            unit = jnp.concatenate([unit] * (sub // unit.shape[0]), axis=0)
            term = x_ref[f, rows] * unit
            total = term if total is None else total + term
        xsend[cut, step] = total

    if order is None:
        repeat(devices - 1, lambda s: idx_copy(s).wait_recv())
    for cut in range(cuts):

        def select_send(step, cut=cut):
            if cut == 0 and order is not None:
                idx_copy(step).wait_recv()
            select(step, cut)
            hop(step, cut).start()

        each_peer(select_send, (2, 1, 0))

    project(2, v_ref, False)
    project(0, q_ref, False)

    lane_head = lax.broadcasted_iota(jnp.int32, (share, breadth), 1) // HD

    def attend(blocks, key_rows, values):
        nothing = jnp.zeros((share, breadth), jnp.bfloat16)
        stacked = jnp.concatenate(
            [
                jnp.where(lane_head == h, blocks[p], nothing)
                for p in range(parts)
                for h in range(heads)
            ],
            axis=0,
        )
        scores = lax.dot_general(
            key_rows, stacked, (((1,), (1,)), ((), ())), preferred_element_type=jnp.float32
        )
        peak = jnp.max(scores, axis=0, keepdims=True)
        lifted = jnp.exp(scores - peak)
        total = jnp.sum(lifted, axis=0, keepdims=True)
        shares = (lifted * (1.0 / total)).astype(jnp.bfloat16)
        lse = peak + jnp.log(total)
        wide = lax.dot_general(
            shares, values, (((0,), (0,)), ((), ())), preferred_element_type=jnp.float32
        )
        outs = []
        for p in range(parts):
            rows = wide[p * lanes : (p + 1) * lanes]
            shown = rows[:share]
            for h in range(1, heads):
                shown = jnp.where(lane_head == h, rows[h * share : (h + 1) * share], shown)
            outs.append(shown.astype(jnp.bfloat16))
        return outs, [lse[:, p * lanes : (p + 1) * lanes] for p in range(parts)]

    def self_body(f, carry):
        queries = q_ref[f]
        outs, lses = attend(
            [queries[p * share : (p + 1) * share] for p in range(parts)], k_ref[f], v_ref[f]
        )
        for p in range(parts):
            self_send[p, f] = outs[p]
            self_lse[p, pl.ds(f, 1)] = lses[p]
        return carry

    part_frames = frames_here // 2
    def self_part(i):
        lax.fori_loop(i * part_frames, (i + 1) * part_frames, self_body, 0, unroll=4)

    self_part(0)

    own = info[0, here]
    ks[here] = k_ref[own]
    vs[here] = v_ref[own]
    queries = q_ref[own]
    for cut in range(cuts):
        for p in range(parts):
            low = p * share + cut * sub
            qs[here, (cut * parts + p) * sub : (cut * parts + p + 1) * sub] = queries[low : low + sub]

    piece_rows = parts * sub

    def project_piece(cut):
        rows = pl.ds(cut * piece_rows, piece_rows)

        def one(slots, count):
            taken = xs[cut, slots].reshape(count * piece_rows, width)
            for which, target in ((1, ks), (2, vs), (0, qs)):
                made = jnp.dot(taken, w_ref[which], preferred_element_type=jnp.float32)
                if which == 0:
                    made = made * (HD ** -0.5)
                target[slots, rows] = made.astype(jnp.bfloat16).reshape(count, piece_rows, breadth)

        if small:
            one(pl.ds(0, devices - 1), devices - 1)
        else:
            repeat(devices - 1, lambda step: one(pl.ds(step, 1), 1))

    for cut in range(cuts):

        def arrive(step, cut=cut):
            hop(step, cut).wait_recv()
            g_copy(step, cut, 0).start()
            g_copy(step, cut, 1).start()

        each_peer(arrive, (0, 2, 1))

    for cut in range(cuts):

        def forward(step, cut=cut):
            g_copy(step, cut, 1).wait_recv()
            g_copy(step, cut, 2).start()

        each_peer(forward, (0, 2, 1))
        if cut == 0:
            w_copy(1).wait_recv()
            w_copy(2).start()
            w_copy(3).start()
            self_part(1)

    def m_start(i):
        for j in (1, 2, 3):
            m_copy(j, i).start()

    m_start(0)
    m_start(1)
    for j in (1, 2, 3):
        ml_copy(j).start()
    self_recv[part] = self_send[part]
    self_lse_recv[part] = self_lse[part]

    for cut in range(cuts):

        def whole(step, cut=cut):
            g_copy(step, cut, 0).wait_recv()
            g_copy(step, cut, 2).wait_recv()

        each_peer(whole, (0, 2, 1))
        project_piece(cut)

    def attend_slot(slot):
        partner = info[1, slot]
        queries = qs[slot]
        blocks = [
            jnp.concatenate(
                [
                    queries[(cut * parts + p) * sub : (cut * parts + p + 1) * sub]
                    for cut in range(cuts)
                ],
                axis=0,
            )
            for p in range(parts)
        ]
        outs, lses = attend(blocks, ks[partner], vs[partner])
        for p in range(parts):
            pair_send[slot, p] = outs[p]
            pair_lse[slot, p] = lses[p]

    def slot_send(step):
        attend_slot(slot_to(step))
        for j in (0, 1, 2, 3):
            for copy in pair_copies(step, j):
                copy.start()

    each_peer(slot_send, (1, 2, 0))
    attend_slot(here)
    for j in range(1, parts):
        for copy in pair_copies(here, j):
            copy.start()
    pair_recv[here, part] = pair_send[here, part]
    pair_lse_recv[here, part] = pair_lse[here, part]

    w_copy(2).wait_recv()
    w_copy(4).start()
    w_copy(0).wait_recv()
    for j in range(1, parts):
        for i in range(2):
            m_copy(j, i).wait_recv()
        ml_copy(j).wait_recv()
    w_copy(3).wait_recv()
    w_copy(4).wait_recv()

    def pairs_in(step):
        for j in range(parts):
            for copy in pair_copies(step, j):
                copy.wait_recv()

    for j in range(1, parts):
        for copy in pair_copies(here, j):
            copy.wait_recv()
    repeat(devices - 1, pairs_in)

    row_frame = lax.broadcasted_iota(jnp.int32, (frames_here, lanes), 0)
    tables = []
    for g in range(parts):
        own_lse = self_lse_recv[g]

        def lifted_lse(owner, g=g):
            row = jnp.broadcast_to(pair_lse_recv[owner, g], (frames_here, lanes))
            return jnp.where(idx_recv[owner] == row_frame, row, -jnp.inf)

        peak = lax.fori_loop(
            0, devices, lambda o, p: jnp.maximum(p, lifted_lse(o)), own_lse, unroll=small
        )
        own_weight = jnp.exp(own_lse - peak)
        den = lax.fori_loop(
            0, devices, lambda o, d: d + jnp.exp(lifted_lse(o) - peak), own_weight, unroll=small
        )
        inverse = 1.0 / den
        tables.append(own_weight * inverse)

        def slot_weight(owner, g=g, peak=peak, inverse=inverse):
            weight = jnp.exp(lifted_lse(owner) - peak) * inverse
            slot_weights[owner, pl.ds(g, 1)] = jnp.sum(weight, axis=0, keepdims=True)

        repeat(devices, slot_weight)

    low_lane = lax.broadcasted_iota(jnp.int32, (share, 2 * HD), 1) < HD

    def spread(columns, c):
        picked = [
            jnp.broadcast_to(columns[h * share : (h + 1) * share, c : c + 1], (share, 2 * HD))
            for h in range(heads)
        ]
        return jnp.concatenate(
            [jnp.where(low_lane, picked[h], picked[h + 1]) for h in range(0, heads, 2)], axis=1
        )

    def scale_slot(owner):
        columns = jnp.transpose(slot_weights[owner])
        for g in range(parts):
            scaled[owner, :, g * breadth : (g + 1) * breadth] = (
                pair_recv[owner, g].astype(jnp.float32) * spread(columns, g)
            )

    repeat(devices, scale_slot)

    own_columns = jnp.transpose(jnp.concatenate(tables, axis=0))
    for f in range(frames_here):
        for g in range(parts):
            state = self_recv[g, f].astype(jnp.float32) * spread(own_columns, g * frames_here + f)

            def add(owner, state, g=g, f=f):
                hit = idx_recv[owner] == f
                hit = jnp.concatenate([hit] * (share // hit.shape[0]), axis=0)
                hit = jnp.concatenate([hit] * (breadth // hit.shape[1]), axis=1)
                return state + jnp.where(hit, scaled[owner, :, g * breadth : (g + 1) * breadth], 0.0)

            state = lax.fori_loop(0, devices, add, state, unroll=small)
            merged[f * share : (f + 1) * share, g * breadth : (g + 1) * breadth] = state.astype(
                jnp.bfloat16
            )

    for n in range(0, width, 256):
        total = None
        for g in range(parts):
            term = jnp.dot(
                merged[:, g * breadth : (g + 1) * breadth], wall[g, :, n : n + 256],
                preferred_element_type=jnp.float32,
            )
            total = term if total is None else total + term
        out_ref[:, :, n : n + 256] = total.astype(jnp.bfloat16).reshape(frames_here, share, 256)

    repeat(devices - 1, lambda s: idx_copy(s).wait_send())

    def sent(step):
        for cut in range(cuts):
            hop(step, cut).wait_send()
            for kind in range(3):
                g_copy(step, cut, kind).wait_send()
        for j in range(parts):
            for copy in pair_copies(step, j):
                copy.wait_send()

    repeat(devices - 1, sent)
    for j in range(1, parts):
        for i in range(2):
            m_copy(j, i).wait_send()
        ml_copy(j).wait_send()
        for copy in pair_copies(here, j):
            copy.wait_send()
    for kind in range(5):
        w_copy(kind).wait_send()


def local(tokens, w_qkv, w_out, pair_slots):
    frames_here, length, width = tokens.shape
    breadth = w_qkv.shape[2]
    devices = lax.axis_size("frames")
    parts = lax.axis_size("heads")
    groups = lax.axis_size("groups")
    cap = pair_slots.shape[0]
    share = length // parts
    lanes = breadth // HD * share
    cuts = 2
    bf, f32 = jnp.bfloat16, jnp.float32
    smem = pl.BlockSpec(memory_space=pltpu.SMEM)
    vm = pl.BlockSpec(memory_space=pltpu.VMEM)
    hbm = pl.BlockSpec(memory_space=pl.ANY)
    dma = pltpu.SemaphoreType.DMA
    vmem = pltpu.VMEM
    return pl.pallas_call(
        functools.partial(kernel, devices, parts, groups, cap),
        out_shape=pltpu.VMEM((frames_here, share, width), bf),
        in_specs=[smem, hbm, hbm, hbm],
        out_specs=vm,
        scratch_shapes=[
            pltpu.SMEM((2, devices), jnp.int32),
            vmem((frames_here, length, width), bf),
            vmem((3, width, breadth), bf),
            vmem((parts, breadth, width), bf),
        ]
        + [vmem((frames_here, length, breadth), bf)] * 3
        + [vmem((devices, frames_here, lanes), jnp.int32)] * 2
        + [
            vmem((cuts, devices - 1, share // cuts, width), bf),
            vmem((cuts, devices - 1, length // cuts, width), bf),
        ]
        + [vmem((devices, length, breadth), bf)] * 3
        + [vmem((parts, frames_here, share, breadth), bf)] * 2
        + [vmem((parts, frames_here, lanes), f32)] * 2
        + [vmem((devices, parts, share, breadth), bf)] * 2
        + [vmem((devices, parts, 1, lanes), f32)] * 2
        + [
            vmem((devices, parts, lanes), f32),
            vmem((devices, share, width), f32),
            vmem((frames_here * share, width), bf),
        ]
        + [dma((frames_here * length // 256,)), dma((3,)), dma]
        + [dma((devices - 1,))] * 2
        + [dma((cuts, devices - 1))] * 2
        + [dma((cuts, devices - 1, 3))] * 2
        + [dma((parts - 1, 2))] * 2
        + [dma((parts - 1,))] * 2
        + [dma((devices, parts))] * 4
        + [dma((5,))] * 2,
        compiler_params=pltpu.CompilerParams(
            collective_id=0, has_side_effects=True, vmem_limit_bytes=60 * 1024 * 1024
        ),
    )(
        pair_slots,
        tokens,
        jnp.transpose(w_qkv, (1, 0, 2)),
        w_out,
    )


def solution(mesh):
    placed = (
        P(("groups", "frames"), None, None),
        P(None, None, "heads"),
        P("heads", None),
        P(("groups", "frames"), None),
    )
    return jax.shard_map(
        local,
        mesh=mesh,
        in_specs=placed,
        out_specs=P(("groups", "frames"), "heads", None),
        check_vma=False,
    )
```

```python
import functools

import jax
import jax.numpy as jnp
from jax import lax
from jax.experimental import pallas as pl
from jax.experimental.pallas import tpu as pltpu
from jax.sharding import PartitionSpec as P

HD = 64
MESH = pl.DeviceIdType.MESH


def repeat(count, body):
    if count <= 8:
        for step in range(count):
            body(step)
    else:

        def step_body(step, carry):
            body(step)
            return carry

        lax.fori_loop(0, count, step_body, 0)


def kernel(
    devices, parts, groups, cap,
    pairs_hbm, x_hbm, w_hbm, wo_hbm, out_ref,
    pairs_ref, info, x_ref, w_ref, wall, q_ref, k_ref, v_ref,
    idx_send, idx_recv, xsend, xs, qs, ks, vs,
    self_send, self_recv, self_lse, self_lse_recv,
    pair_send, pair_recv, pair_lse, pair_lse_recv,
    slot_weights, scaled, merged,
    pairs_sem, x_sem, w_sem, wo_sem, i_send, i_recv, h_send, h_recv, g_send, g_recv,
    m_send, m_recv, ml_send, ml_recv, p_send, p_recv, pl_send, pl_recv, o_send, o_recv,
):
    me = lax.axis_index("frames")
    part = lax.axis_index("heads")
    group = lax.axis_index("groups")
    frames_here, length, breadth = q_ref.shape
    width = x_ref.shape[2]
    heads = breadth // HD
    share = length // parts
    lanes = heads * share
    per = 256 // length
    chunks = frames_here // per
    half = breadth // 2
    cuts = 2
    sub = share // cuts
    here = devices - 1
    small = devices <= 8

    def peer(step):
        if devices == 4:
            low = lax.rem(me, 2)
            high = lax.div(me, 2)
            return (
                2 * high + 1 - low,
                2 * (1 - high) + low,
                3 - me,
            )[step]
        return lax.rem(me + step + 1, devices)

    def source(step):
        if devices == 4:
            return peer(step)
        return lax.rem(me + devices - step - 1, devices)

    def slot_to(step):
        return step if devices == 4 else devices - 2 - step

    def slot_of(home):
        if devices == 4:
            low = jnp.abs(lax.rem(home, 2) - lax.rem(me, 2))
            high = jnp.abs(lax.div(home, 2) - lax.div(me, 2))
            return lax.rem(low + 2 * high + 3, 4)
        return lax.rem(me - home - 1 + 2 * devices, devices)

    order = (1, 2, 0) if devices == 4 else None

    def each_peer(body, order=order):
        if devices != 4:
            repeat(devices - 1, body)
        else:
            for step in order:
                body(step)

    def head_peer(step):
        return lax.rem(part + step, parts)

    mate = part + 1 - 2 * lax.rem(part, 2)
    across = lax.rem(part + 2, parts)

    def own_rows(block):
        return pl.ds(pl.multiple_of(block * sub, sub), sub)

    barrier = pltpu.get_barrier_semaphore()

    def greet(step):
        pl.semaphore_signal(
            barrier, inc=1, device_id={"frames": peer(step)}, device_id_type=MESH
        )

    repeat(devices - 1, greet)
    for j in range(1, parts):
        pl.semaphore_signal(
            barrier, inc=1, device_id={"heads": head_peer(j)}, device_id_type=MESH
        )
    for j in range(1, groups):
        pl.semaphore_signal(
            barrier, inc=1, device_id={"groups": lax.rem(group + j, groups)}, device_id_type=MESH
        )

    def x_copy(i):
        rows = pl.ds(i * per, per)
        return pltpu.make_async_copy(x_hbm.at[rows], x_ref.at[rows], x_sem.at[i])

    def w_load(which):
        return pltpu.make_async_copy(w_hbm.at[which], w_ref.at[which], w_sem.at[which])

    pairs_load = pltpu.make_async_copy(pairs_hbm, pairs_ref, pairs_sem)
    pairs_load.start()
    wo_load = pltpu.make_async_copy(wo_hbm, wall.at[part], wo_sem)
    w_load(1).start()
    for i in range(chunks):
        x_copy(i).start()
    wo_load.start()
    w_load(2).start()
    w_load(0).start()

    def look(slot):
        home = me if isinstance(slot, int) and slot == here else source(slot)
        low = home * frames_here
        frame = jnp.int32(-1)
        partner = jnp.int32(0) + me
        for row in range(cap):
            a = pairs_ref[row, 0]
            b = pairs_ref[row, 1]
            hit_a = (a >= low) & (a < low + frames_here)
            hit_b = (b >= low) & (b < low + frames_here)
            frame = jnp.where(hit_a, a - low, jnp.where(hit_b, b - low, frame))
            partner = jnp.where(
                hit_a, lax.div(b, jnp.int32(frames_here)),
                jnp.where(hit_b, lax.div(a, jnp.int32(frames_here)), partner),
            )
        info[0, slot] = jnp.maximum(frame, 0)
        info[1, slot] = slot_of(partner)
        idx_send[slot] = jnp.full(idx_send.shape[1:], frame, jnp.int32)

    pairs_load.wait()
    repeat(devices - 1, look)
    look(here)
    idx_recv[here] = idx_send[here]

    def idx_copy(step):
        to = peer(step)
        return pltpu.make_async_remote_copy(
            idx_send.at[slot_to(step)], idx_recv.at[step], i_send.at[step], i_recv.at[step],
            device_id={"frames": to}, device_id_type=MESH,
        )

    def hop(step, cut):
        return pltpu.make_async_remote_copy(
            xsend.at[cut, step], xs.at[cut, step, own_rows(part)],
            h_send.at[cut, step], h_recv.at[cut, step],
            device_id={"frames": peer(step)}, device_id_type=MESH,
        )

    def g_copy(step, cut, kind):
        piece = xs.at[cut, step, own_rows(across if kind == 2 else part)]
        return pltpu.make_async_remote_copy(
            piece, piece, g_send.at[cut, step, kind], g_recv.at[cut, step, kind],
            device_id={"heads": across if kind == 1 else mate}, device_id_type=MESH,
        )

    first_half = pl.ds(pl.multiple_of(group * half, half), half)
    second_half = pl.ds(pl.multiple_of((1 - group) * half, half), half)

    def w_copy(kind):
        piece = (
            wall.at[part],
            wall.at[part, first_half],
            wall.at[across, first_half],
            wall.at[across, first_half],
            wall.at[across, second_half],
        )[kind]
        target = (
            {"heads": mate},
            {"heads": across},
            {"groups": 1 - group},
            {"heads": mate},
            {"heads": mate},
        )[kind]
        return pltpu.make_async_remote_copy(
            piece, piece, o_send.at[kind], o_recv.at[kind],
            device_id=target, device_id_type=MESH,
        )

    def m_copy(step, i):
        to = head_peer(step)
        frames = pl.ds(i * (frames_here // 2), frames_here // 2)
        return pltpu.make_async_remote_copy(
            self_send.at[to, frames], self_recv.at[part, frames],
            m_send.at[step - 1, i], m_recv.at[step - 1, i],
            device_id={"heads": to}, device_id_type=MESH,
        )

    def ml_copy(step):
        to = head_peer(step)
        return pltpu.make_async_remote_copy(
            self_lse.at[to], self_lse_recv.at[part], ml_send.at[step - 1], ml_recv.at[step - 1],
            device_id={"heads": to}, device_id_type=MESH,
        )

    def pair_copies(step, j):
        own = isinstance(step, int) and step == devices - 1
        slot = step if own else slot_to(step)
        to = head_peer(j)
        where = {"heads": to} if own else {"frames": peer(step), "heads": to}
        return (
            pltpu.make_async_remote_copy(
                pair_send.at[slot, to], pair_recv.at[step, part],
                p_send.at[step, j], p_recv.at[step, j],
                device_id=where, device_id_type=MESH,
            ),
            pltpu.make_async_remote_copy(
                pair_lse.at[slot, to], pair_lse_recv.at[step, part],
                pl_send.at[step, j], pl_recv.at[step, j],
                device_id=where, device_id_type=MESH,
            ),
        )

    pl.semaphore_wait(barrier, devices - 1 + parts - 1 + groups - 1)
    repeat(devices - 1, lambda s: idx_copy(s).start())
    wo_load.wait()
    w_copy(1).start()
    w_copy(0).start()

    def project(which, target, first):
        w_load(which).wait()

        def body(i, carry):
            if first:
                x_copy(i).wait()
            rows = x_ref[pl.ds(i * per, per)].reshape(per * length, width)
            made = jnp.dot(rows, w_ref[which], preferred_element_type=jnp.float32)
            if which == 0:
                made = made * (HD ** -0.5)
            target[pl.ds(i * per, per)] = made.astype(jnp.bfloat16).reshape(per, length, breadth)
            return carry

        lax.fori_loop(0, chunks, body, 0)

    project(1, k_ref, True)

    def select(step, cut):
        asked = idx_recv[slot_to(step)]
        rows = pl.ds(pl.multiple_of(part * share + cut * sub, sub), sub)
        total = None
        for f in range(frames_here):
            unit = jnp.where(asked == f, 1.0, 0.0)
            unit = jnp.concatenate([unit, unit], axis=0).astype(jnp.bfloat16)
            unit = jnp.concatenate([unit] * (width // unit.shape[1]), axis=1)
            unit = jnp.concatenate([unit] * (sub // unit.shape[0]), axis=0)
            term = x_ref[f, rows] * unit
            total = term if total is None else total + term
        xsend[cut, step] = total

    if order is None:
        repeat(devices - 1, lambda s: idx_copy(s).wait_recv())
    for cut in range(cuts):

        def select_send(step, cut=cut):
            if cut == 0 and order is not None:
                idx_copy(step).wait_recv()
            select(step, cut)
            hop(step, cut).start()

        each_peer(select_send, (2, 0, 1))

    project(2, v_ref, False)
    project(0, q_ref, False)

    lane_head = lax.broadcasted_iota(jnp.int32, (share, breadth), 1) // HD

    def attend(blocks, key_rows, values):
        nothing = jnp.zeros((share, breadth), jnp.bfloat16)
        stacked = jnp.concatenate(
            [
                jnp.where(lane_head == h, blocks[p], nothing)
                for p in range(parts)
                for h in range(heads)
            ],
            axis=0,
        )
        scores = lax.dot_general(
            key_rows, stacked, (((1,), (1,)), ((), ())), preferred_element_type=jnp.float32
        )
        peak = jnp.max(scores, axis=0, keepdims=True)
        lifted = jnp.exp(scores - peak)
        total = jnp.sum(lifted, axis=0, keepdims=True)
        shares = (lifted * (1.0 / total)).astype(jnp.bfloat16)
        lse = peak + jnp.log(total)
        wide = lax.dot_general(
            shares, values, (((0,), (0,)), ((), ())), preferred_element_type=jnp.float32
        )
        outs = []
        for p in range(parts):
            rows = wide[p * lanes : (p + 1) * lanes]
            shown = rows[:share]
            for h in range(1, heads):
                shown = jnp.where(lane_head == h, rows[h * share : (h + 1) * share], shown)
            outs.append(shown.astype(jnp.bfloat16))
        return outs, [lse[:, p * lanes : (p + 1) * lanes] for p in range(parts)]

    def self_body(f, carry):
        queries = q_ref[f]
        outs, lses = attend(
            [queries[p * share : (p + 1) * share] for p in range(parts)], k_ref[f], v_ref[f]
        )
        for p in range(parts):
            self_send[p, f] = outs[p]
            self_lse[p, pl.ds(f, 1)] = lses[p]
        return carry

    part_frames = frames_here // 2
    def self_part(i):
        lax.fori_loop(i * part_frames, (i + 1) * part_frames, self_body, 0, unroll=4)

    self_part(0)

    own = info[0, here]
    ks[here] = k_ref[own]
    vs[here] = v_ref[own]
    queries = q_ref[own]
    for cut in range(cuts):
        for p in range(parts):
            low = p * share + cut * sub
            qs[here, (cut * parts + p) * sub : (cut * parts + p + 1) * sub] = queries[low : low + sub]

    piece_rows = parts * sub

    def project_piece(cut):
        rows = pl.ds(cut * piece_rows, piece_rows)

        def one(slots, count):
            taken = xs[cut, slots].reshape(count * piece_rows, width)
            for which, target in ((1, ks), (2, vs), (0, qs)):
                made = jnp.dot(taken, w_ref[which], preferred_element_type=jnp.float32)
                if which == 0:
                    made = made * (HD ** -0.5)
                target[slots, rows] = made.astype(jnp.bfloat16).reshape(count, piece_rows, breadth)

        if small:
            one(pl.ds(0, devices - 1), devices - 1)
        else:
            repeat(devices - 1, lambda step: one(pl.ds(step, 1), 1))

    for cut in range(cuts):

        def arrive(step, cut=cut):
            hop(step, cut).wait_recv()
            g_copy(step, cut, 0).start()
            g_copy(step, cut, 1).start()

        each_peer(arrive, (0, 2, 1))

    for cut in range(cuts):

        def forward(step, cut=cut):
            g_copy(step, cut, 1).wait_recv()
            g_copy(step, cut, 2).start()

        each_peer(forward, (0, 2, 1))
        if cut == 0:
            w_copy(1).wait_recv()
            w_copy(2).start()
            w_copy(3).start()
            self_part(1)

    def m_start(i):
        for j in (1, 2, 3):
            m_copy(j, i).start()

    m_start(0)
    m_start(1)
    for j in (1, 2, 3):
        ml_copy(j).start()
    self_recv[part] = self_send[part]
    self_lse_recv[part] = self_lse[part]

    for cut in range(cuts):

        def whole(step, cut=cut):
            g_copy(step, cut, 0).wait_recv()
            g_copy(step, cut, 2).wait_recv()

        each_peer(whole, (0, 2, 1))
        project_piece(cut)

    def attend_slot(slot):
        partner = info[1, slot]
        queries = qs[slot]
        blocks = [
            jnp.concatenate(
                [
                    queries[(cut * parts + p) * sub : (cut * parts + p + 1) * sub]
                    for cut in range(cuts)
                ],
                axis=0,
            )
            for p in range(parts)
        ]
        outs, lses = attend(blocks, ks[partner], vs[partner])
        for p in range(parts):
            pair_send[slot, p] = outs[p]
            pair_lse[slot, p] = lses[p]

    def slot_send(step):
        attend_slot(slot_to(step))
        for j in (0, 1, 2, 3):
            for copy in pair_copies(step, j):
                copy.start()

    each_peer(slot_send, (1, 2, 0))
    attend_slot(here)
    for j in range(1, parts):
        for copy in pair_copies(here, j):
            copy.start()
    pair_recv[here, part] = pair_send[here, part]
    pair_lse_recv[here, part] = pair_lse[here, part]

    w_copy(2).wait_recv()
    w_copy(4).start()
    w_copy(0).wait_recv()
    for j in range(1, parts):
        for i in range(2):
            m_copy(j, i).wait_recv()
        ml_copy(j).wait_recv()
    w_copy(3).wait_recv()
    w_copy(4).wait_recv()

    def pairs_in(step):
        for j in range(parts):
            for copy in pair_copies(step, j):
                copy.wait_recv()

    for j in range(1, parts):
        for copy in pair_copies(here, j):
            copy.wait_recv()
    repeat(devices - 1, pairs_in)

    row_frame = lax.broadcasted_iota(jnp.int32, (frames_here, lanes), 0)
    tables = []
    for g in range(parts):
        own_lse = self_lse_recv[g]

        def lifted_lse(owner, g=g):
            row = jnp.broadcast_to(pair_lse_recv[owner, g], (frames_here, lanes))
            return jnp.where(idx_recv[owner] == row_frame, row, -jnp.inf)

        peak = lax.fori_loop(
            0, devices, lambda o, p: jnp.maximum(p, lifted_lse(o)), own_lse, unroll=small
        )
        own_weight = jnp.exp(own_lse - peak)
        den = lax.fori_loop(
            0, devices, lambda o, d: d + jnp.exp(lifted_lse(o) - peak), own_weight, unroll=small
        )
        inverse = 1.0 / den
        tables.append(own_weight * inverse)

        def slot_weight(owner, g=g, peak=peak, inverse=inverse):
            weight = jnp.exp(lifted_lse(owner) - peak) * inverse
            slot_weights[owner, pl.ds(g, 1)] = jnp.sum(weight, axis=0, keepdims=True)

        repeat(devices, slot_weight)

    low_lane = lax.broadcasted_iota(jnp.int32, (share, 2 * HD), 1) < HD

    def spread(columns, c):
        picked = [
            jnp.broadcast_to(columns[h * share : (h + 1) * share, c : c + 1], (share, 2 * HD))
            for h in range(heads)
        ]
        return jnp.concatenate(
            [jnp.where(low_lane, picked[h], picked[h + 1]) for h in range(0, heads, 2)], axis=1
        )

    def scale_slot(owner):
        columns = jnp.transpose(slot_weights[owner])
        for g in range(parts):
            scaled[owner, :, g * breadth : (g + 1) * breadth] = (
                pair_recv[owner, g].astype(jnp.float32) * spread(columns, g)
            )

    repeat(devices, scale_slot)

    own_columns = jnp.transpose(jnp.concatenate(tables, axis=0))
    for f in range(frames_here):
        for g in range(parts):
            state = self_recv[g, f].astype(jnp.float32) * spread(own_columns, g * frames_here + f)

            def add(owner, state, g=g, f=f):
                hit = idx_recv[owner] == f
                hit = jnp.concatenate([hit] * (share // hit.shape[0]), axis=0)
                hit = jnp.concatenate([hit] * (breadth // hit.shape[1]), axis=1)
                return state + jnp.where(hit, scaled[owner, :, g * breadth : (g + 1) * breadth], 0.0)

            state = lax.fori_loop(0, devices, add, state, unroll=small)
            merged[f * share : (f + 1) * share, g * breadth : (g + 1) * breadth] = state.astype(
                jnp.bfloat16
            )

    for n in range(0, width, 256):
        total = None
        for g in range(parts):
            term = jnp.dot(
                merged[:, g * breadth : (g + 1) * breadth], wall[g, :, n : n + 256],
                preferred_element_type=jnp.float32,
            )
            total = term if total is None else total + term
        out_ref[:, :, n : n + 256] = total.astype(jnp.bfloat16).reshape(frames_here, share, 256)

    repeat(devices - 1, lambda s: idx_copy(s).wait_send())

    def sent(step):
        for cut in range(cuts):
            hop(step, cut).wait_send()
            for kind in range(3):
                g_copy(step, cut, kind).wait_send()
        for j in range(parts):
            for copy in pair_copies(step, j):
                copy.wait_send()

    repeat(devices - 1, sent)
    for j in range(1, parts):
        for i in range(2):
            m_copy(j, i).wait_send()
        ml_copy(j).wait_send()
        for copy in pair_copies(here, j):
            copy.wait_send()
    for kind in range(5):
        w_copy(kind).wait_send()


def local(tokens, w_qkv, w_out, pair_slots):
    frames_here, length, width = tokens.shape
    breadth = w_qkv.shape[2]
    devices = lax.axis_size("frames")
    parts = lax.axis_size("heads")
    groups = lax.axis_size("groups")
    cap = pair_slots.shape[0]
    share = length // parts
    lanes = breadth // HD * share
    cuts = 2
    bf, f32 = jnp.bfloat16, jnp.float32
    vm = pl.BlockSpec(memory_space=pltpu.VMEM)
    hbm = pl.BlockSpec(memory_space=pl.ANY)
    dma = pltpu.SemaphoreType.DMA
    vmem = pltpu.VMEM
    return pl.pallas_call(
        functools.partial(kernel, devices, parts, groups, cap),
        out_shape=pltpu.VMEM((frames_here, share, width), bf),
        in_specs=[hbm] * 4,
        out_specs=vm,
        scratch_shapes=[
            pltpu.SMEM(pair_slots.shape, jnp.int32),
            pltpu.SMEM((2, devices), jnp.int32),
            vmem((frames_here, length, width), bf),
            vmem((3, width, breadth), bf),
            vmem((parts, breadth, width), bf),
        ]
        + [vmem((frames_here, length, breadth), bf)] * 3
        + [vmem((devices, frames_here, lanes), jnp.int32)] * 2
        + [
            vmem((cuts, devices - 1, share // cuts, width), bf),
            vmem((cuts, devices - 1, length // cuts, width), bf),
        ]
        + [vmem((devices, length, breadth), bf)] * 3
        + [vmem((parts, frames_here, share, breadth), bf)] * 2
        + [vmem((parts, frames_here, lanes), f32)] * 2
        + [vmem((devices, parts, share, breadth), bf)] * 2
        + [vmem((devices, parts, 1, lanes), f32)] * 2
        + [
            vmem((devices, parts, lanes), f32),
            vmem((devices, share, width), f32),
            vmem((frames_here * share, width), bf),
        ]
        + [dma, dma((frames_here * length // 256,)), dma((3,)), dma]
        + [dma((devices - 1,))] * 2
        + [dma((cuts, devices - 1))] * 2
        + [dma((cuts, devices - 1, 3))] * 2
        + [dma((parts - 1, 2))] * 2
        + [dma((parts - 1,))] * 2
        + [dma((devices, parts))] * 4
        + [dma((5,))] * 2,
        compiler_params=pltpu.CompilerParams(
            collective_id=0, has_side_effects=True, vmem_limit_bytes=60 * 1024 * 1024
        ),
    )(
        pair_slots,
        tokens,
        jnp.transpose(w_qkv, (1, 0, 2)),
        w_out,
    )


def solution(mesh):
    placed = (
        P(("groups", "frames"), None, None),
        P(None, None, "heads"),
        P("heads", None),
        P(("groups", "frames"), None),
    )
    return jax.shard_map(
        local,
        mesh=mesh,
        in_specs=placed,
        out_specs=P(("groups", "frames"), "heads", None),
        check_vma=False,
    )
```

```python
import functools

import jax
import jax.numpy as jnp
from jax import lax
from jax.experimental import pallas as pl
from jax.experimental.pallas import tpu as pltpu
from jax.sharding import PartitionSpec as P

HD = 64
MESH = pl.DeviceIdType.MESH


def repeat(count, body):
    if count <= 8:
        for step in range(count):
            body(step)
    else:

        def step_body(step, carry):
            body(step)
            return carry

        lax.fori_loop(0, count, step_body, 0)


def kernel(
    devices, parts, groups, cap,
    pairs_hbm, x_hbm, w_hbm, wo_hbm, out_ref,
    pairs_ref, info, x_ref, w_ref, wall, q_ref, k_ref, v_ref,
    idx_send, idx_recv, xsend, xs, qs, ks, vs,
    self_send, self_recv, self_lse, self_lse_recv,
    pair_send, pair_recv, pair_lse, pair_lse_recv,
    slot_weights, scaled, merged, base, slot_rows,
    pairs_sem, x_sem, w_sem, wo_sem, i_send, i_recv, h_send, h_recv, g_send, g_recv,
    m_send, m_recv, ml_send, ml_recv, p_send, p_recv, pl_send, pl_recv, o_send, o_recv,
):
    me = lax.axis_index("frames")
    part = lax.axis_index("heads")
    group = lax.axis_index("groups")
    frames_here, length, breadth = q_ref.shape
    width = x_ref.shape[2]
    heads = breadth // HD
    share = length // parts
    lanes = heads * share
    per = 256 // length
    chunks = frames_here // per
    half = breadth // 2
    cuts = 2
    sub = share // cuts
    here = devices - 1
    small = devices <= 8

    def peer(step):
        if devices == 4:
            low = lax.rem(me, 2)
            high = lax.div(me, 2)
            return (
                2 * high + 1 - low,
                2 * (1 - high) + low,
                3 - me,
            )[step]
        return lax.rem(me + step + 1, devices)

    def source(step):
        if devices == 4:
            return peer(step)
        return lax.rem(me + devices - step - 1, devices)

    def slot_to(step):
        return step if devices == 4 else devices - 2 - step

    def slot_of(home):
        if devices == 4:
            low = jnp.abs(lax.rem(home, 2) - lax.rem(me, 2))
            high = jnp.abs(lax.div(home, 2) - lax.div(me, 2))
            return lax.rem(low + 2 * high + 3, 4)
        return lax.rem(me - home - 1 + 2 * devices, devices)

    order = (1, 2, 0) if devices == 4 else None

    def each_peer(body, order=order):
        if devices != 4:
            repeat(devices - 1, body)
        else:
            for step in order:
                body(step)

    def head_peer(step):
        return lax.rem(part + step, parts)

    mate = part + 1 - 2 * lax.rem(part, 2)
    across = lax.rem(part + 2, parts)

    def own_rows(block):
        return pl.ds(pl.multiple_of(block * sub, sub), sub)

    barrier = pltpu.get_barrier_semaphore()

    def greet(step):
        pl.semaphore_signal(
            barrier, inc=1, device_id={"frames": peer(step)}, device_id_type=MESH
        )

    repeat(devices - 1, greet)
    for j in range(1, parts):
        pl.semaphore_signal(
            barrier, inc=1, device_id={"heads": head_peer(j)}, device_id_type=MESH
        )
    for j in range(1, groups):
        pl.semaphore_signal(
            barrier, inc=1, device_id={"groups": lax.rem(group + j, groups)}, device_id_type=MESH
        )

    def x_copy(i):
        rows = pl.ds(i * per, per)
        return pltpu.make_async_copy(x_hbm.at[rows], x_ref.at[rows], x_sem.at[i])

    def w_load(which):
        return pltpu.make_async_copy(w_hbm.at[which], w_ref.at[which], w_sem.at[which])

    pairs_load = pltpu.make_async_copy(pairs_hbm, pairs_ref, pairs_sem)
    pairs_load.start()
    wo_load = pltpu.make_async_copy(wo_hbm, wall.at[part], wo_sem)
    w_load(1).start()
    for i in range(chunks):
        x_copy(i).start()
    wo_load.start()
    w_load(2).start()
    w_load(0).start()

    def look(slot):
        home = me if isinstance(slot, int) and slot == here else source(slot)
        low = home * frames_here
        frame = jnp.int32(-1)
        partner = jnp.int32(0) + me
        for row in range(cap):
            a = pairs_ref[row, 0]
            b = pairs_ref[row, 1]
            hit_a = (a >= low) & (a < low + frames_here)
            hit_b = (b >= low) & (b < low + frames_here)
            frame = jnp.where(hit_a, a - low, jnp.where(hit_b, b - low, frame))
            partner = jnp.where(
                hit_a, lax.div(b, jnp.int32(frames_here)),
                jnp.where(hit_b, lax.div(a, jnp.int32(frames_here)), partner),
            )
        info[0, slot] = jnp.maximum(frame, 0)
        info[1, slot] = slot_of(partner)
        idx_send[slot] = jnp.full(idx_send.shape[1:], frame, jnp.int32)

    pairs_load.wait()
    repeat(devices - 1, look)
    look(here)
    idx_recv[here] = idx_send[here]

    def idx_copy(step):
        to = peer(step)
        return pltpu.make_async_remote_copy(
            idx_send.at[slot_to(step)], idx_recv.at[step], i_send.at[step], i_recv.at[step],
            device_id={"frames": to}, device_id_type=MESH,
        )

    def hop(step, cut):
        return pltpu.make_async_remote_copy(
            xsend.at[cut, step], xs.at[cut, step, own_rows(part)],
            h_send.at[cut, step], h_recv.at[cut, step],
            device_id={"frames": peer(step)}, device_id_type=MESH,
        )

    def g_copy(step, cut, kind):
        piece = xs.at[cut, step, own_rows(across if kind == 2 else part)]
        return pltpu.make_async_remote_copy(
            piece, piece, g_send.at[cut, step, kind], g_recv.at[cut, step, kind],
            device_id={"heads": across if kind == 1 else mate}, device_id_type=MESH,
        )

    first_half = pl.ds(pl.multiple_of(group * half, half), half)
    second_half = pl.ds(pl.multiple_of((1 - group) * half, half), half)

    def w_copy(kind):
        piece = (
            wall.at[part],
            wall.at[part, first_half],
            wall.at[across, first_half],
            wall.at[across, first_half],
            wall.at[across, second_half],
        )[kind]
        target = (
            {"heads": mate},
            {"heads": across},
            {"groups": 1 - group},
            {"heads": mate},
            {"heads": mate},
        )[kind]
        return pltpu.make_async_remote_copy(
            piece, piece, o_send.at[kind], o_recv.at[kind],
            device_id=target, device_id_type=MESH,
        )

    def m_copy(step, i):
        to = head_peer(step)
        frames = pl.ds(i * (frames_here // 2), frames_here // 2)
        return pltpu.make_async_remote_copy(
            self_send.at[to, frames], self_recv.at[part, frames],
            m_send.at[step - 1, i], m_recv.at[step - 1, i],
            device_id={"heads": to}, device_id_type=MESH,
        )

    def ml_copy(step):
        to = head_peer(step)
        return pltpu.make_async_remote_copy(
            self_lse.at[to], self_lse_recv.at[part], ml_send.at[step - 1], ml_recv.at[step - 1],
            device_id={"heads": to}, device_id_type=MESH,
        )

    def pair_copies(step, j):
        own = isinstance(step, int) and step == devices - 1
        slot = step if own else slot_to(step)
        to = head_peer(j)
        where = {"heads": to} if own else {"frames": peer(step), "heads": to}
        return (
            pltpu.make_async_remote_copy(
                pair_send.at[slot, to], pair_recv.at[step, part],
                p_send.at[step, j], p_recv.at[step, j],
                device_id=where, device_id_type=MESH,
            ),
            pltpu.make_async_remote_copy(
                pair_lse.at[slot, to], pair_lse_recv.at[step, part],
                pl_send.at[step, j], pl_recv.at[step, j],
                device_id=where, device_id_type=MESH,
            ),
        )

    pl.semaphore_wait(barrier, devices - 1 + parts - 1 + groups - 1)
    repeat(devices - 1, lambda s: idx_copy(s).start())
    wo_load.wait()
    w_copy(1).start()
    w_copy(0).start()

    def project(which, target, first):
        w_load(which).wait()

        def body(i, carry):
            if first:
                x_copy(i).wait()
            rows = x_ref[pl.ds(i * per, per)].reshape(per * length, width)
            made = jnp.dot(rows, w_ref[which], preferred_element_type=jnp.float32)
            if which == 0:
                made = made * (HD ** -0.5)
            target[pl.ds(i * per, per)] = made.astype(jnp.bfloat16).reshape(per, length, breadth)
            return carry

        lax.fori_loop(0, chunks, body, 0)

    project(1, k_ref, True)

    def select(step, cut):
        asked = idx_recv[slot_to(step)]
        rows = pl.ds(pl.multiple_of(part * share + cut * sub, sub), sub)
        total = None
        for f in range(frames_here):
            unit = jnp.where(asked == f, 1.0, 0.0)
            unit = jnp.concatenate([unit, unit], axis=0).astype(jnp.bfloat16)
            unit = jnp.concatenate([unit] * (width // unit.shape[1]), axis=1)
            unit = jnp.concatenate([unit] * (sub // unit.shape[0]), axis=0)
            term = x_ref[f, rows] * unit
            total = term if total is None else total + term
        xsend[cut, step] = total

    if order is None:
        repeat(devices - 1, lambda s: idx_copy(s).wait_recv())
    for cut in range(cuts):

        def select_send(step, cut=cut):
            if cut == 0 and order is not None:
                idx_copy(step).wait_recv()
            select(step, cut)
            hop(step, cut).start()

        each_peer(select_send, (2, 0, 1))

    project(2, v_ref, False)
    project(0, q_ref, False)

    lane_head = lax.broadcasted_iota(jnp.int32, (share, breadth), 1) // HD

    def attend(blocks, key_rows, values):
        nothing = jnp.zeros((share, breadth), jnp.bfloat16)
        stacked = jnp.concatenate(
            [
                jnp.where(lane_head == h, blocks[p], nothing)
                for p in range(parts)
                for h in range(heads)
            ],
            axis=0,
        )
        scores = lax.dot_general(
            key_rows, stacked, (((1,), (1,)), ((), ())), preferred_element_type=jnp.float32
        )
        peak = jnp.max(scores, axis=0, keepdims=True)
        lifted = jnp.exp(scores - peak)
        total = jnp.sum(lifted, axis=0, keepdims=True)
        shares = (lifted * (1.0 / total)).astype(jnp.bfloat16)
        lse = peak + jnp.log(total)
        wide = lax.dot_general(
            shares, values, (((0,), (0,)), ((), ())), preferred_element_type=jnp.float32
        )
        outs = []
        for p in range(parts):
            rows = wide[p * lanes : (p + 1) * lanes]
            shown = rows[:share]
            for h in range(1, heads):
                shown = jnp.where(lane_head == h, rows[h * share : (h + 1) * share], shown)
            outs.append(shown.astype(jnp.bfloat16))
        return outs, [lse[:, p * lanes : (p + 1) * lanes] for p in range(parts)]

    def self_body(f, carry):
        queries = q_ref[f]
        outs, lses = attend(
            [queries[p * share : (p + 1) * share] for p in range(parts)], k_ref[f], v_ref[f]
        )
        for p in range(parts):
            self_send[p, f] = outs[p]
            self_lse[p, pl.ds(f, 1)] = lses[p]
        return carry

    part_frames = frames_here // 2
    def self_part(i):
        lax.fori_loop(i * part_frames, (i + 1) * part_frames, self_body, 0, unroll=4)

    self_part(0)

    own = info[0, here]
    ks[here] = k_ref[own]
    vs[here] = v_ref[own]
    queries = q_ref[own]
    for cut in range(cuts):
        for p in range(parts):
            low = p * share + cut * sub
            qs[here, (cut * parts + p) * sub : (cut * parts + p + 1) * sub] = queries[low : low + sub]

    piece_rows = parts * sub

    def project_piece(cut):
        rows = pl.ds(cut * piece_rows, piece_rows)

        def one(slots, count):
            taken = xs[cut, slots].reshape(count * piece_rows, width)
            for which, target in ((1, ks), (2, vs), (0, qs)):
                made = jnp.dot(taken, w_ref[which], preferred_element_type=jnp.float32)
                if which == 0:
                    made = made * (HD ** -0.5)
                target[slots, rows] = made.astype(jnp.bfloat16).reshape(count, piece_rows, breadth)

        if small:
            one(pl.ds(0, devices - 1), devices - 1)
        else:
            repeat(devices - 1, lambda step: one(pl.ds(step, 1), 1))

    def m_start(i):
        for j in (1, 2, 3):
            m_copy(j, i).start()

    for cut in range(cuts):

        def arrive(step, cut=cut):
            hop(step, cut).wait_recv()
            g_copy(step, cut, 0).start()
            g_copy(step, cut, 1).start()

        each_peer(arrive, (0, 2, 1))

    for cut in range(cuts):

        def forward(step, cut=cut):
            g_copy(step, cut, 1).wait_recv()
            g_copy(step, cut, 2).start()

        each_peer(forward, (0, 2, 1))
        if cut == 0:
            w_copy(1).wait_recv()
            w_copy(2).start()
            w_copy(3).start()
            self_part(1)
            m_start(0)

    m_start(1)
    for j in (1, 2, 3):
        ml_copy(j).start()
    self_recv[part] = self_send[part]
    self_lse_recv[part] = self_lse[part]

    for cut in range(cuts):

        def whole(step, cut=cut):
            g_copy(step, cut, 0).wait_recv()
            g_copy(step, cut, 2).wait_recv()

        each_peer(whole, (0, 2, 1))
        project_piece(cut)

    def attend_slot(slot):
        partner = info[1, slot]
        queries = qs[slot]
        blocks = [
            jnp.concatenate(
                [
                    queries[(cut * parts + p) * sub : (cut * parts + p + 1) * sub]
                    for cut in range(cuts)
                ],
                axis=0,
            )
            for p in range(parts)
        ]
        outs, lses = attend(blocks, ks[partner], vs[partner])
        for p in range(parts):
            pair_send[slot, p] = outs[p]
            pair_lse[slot, p] = lses[p]

    def slot_send(step):
        attend_slot(slot_to(step))
        for which in (1, 0):
            for j in range(parts):
                pair_copies(step, j)[which].start()

    each_peer(slot_send, (1, 2, 0))
    attend_slot(here)
    for which in (1, 0):
        for j in range(1, parts):
            pair_copies(here, j)[which].start()
    pair_recv[here, part] = pair_send[here, part]
    pair_lse_recv[here, part] = pair_lse[here, part]

    w_copy(2).wait_recv()
    w_copy(4).start()
    w_copy(0).wait_recv()
    for j in range(1, parts):
        for i in range(2):
            m_copy(j, i).wait_recv()
        ml_copy(j).wait_recv()
    w_copy(3).wait_recv()
    w_copy(4).wait_recv()

    def pairs_sent():
        def pair_sent(step):
            for j in range(parts):
                for copy in pair_copies(step, j):
                    copy.wait_send()

        repeat(devices - 1, pair_sent)
        for j in range(1, parts):
            for copy in pair_copies(here, j):
                copy.wait_send()

    repeat(devices - 1, lambda s: idx_copy(s).wait_send())

    def sent(step):
        for cut in range(cuts):
            hop(step, cut).wait_send()
            for kind in range(3):
                g_copy(step, cut, kind).wait_send()

    repeat(devices - 1, sent)
    for kind in range(5):
        w_copy(kind).wait_send()
    for j in range(1, parts):
        for i in range(2):
            m_copy(j, i).wait_send()
        ml_copy(j).wait_send()
    def pairs_in(which):
        def pair_in(step):
            for j in range(parts):
                pair_copies(step, j)[which].wait_recv()

        for j in range(1, parts):
            pair_copies(here, j)[which].wait_recv()
        repeat(devices - 1, pair_in)

    pairs_in(1)

    row_frame = lax.broadcasted_iota(jnp.int32, (frames_here, lanes), 0)
    tables = []
    for g in range(parts):
        own_lse = self_lse_recv[g]

        def lifted_lse(owner, g=g):
            row = jnp.broadcast_to(pair_lse_recv[owner, g], (frames_here, lanes))
            return jnp.where(idx_recv[owner] == row_frame, row, -jnp.inf)

        peak = lax.fori_loop(
            0, devices, lambda o, p: jnp.maximum(p, lifted_lse(o)), own_lse, unroll=small
        )
        own_weight = jnp.exp(own_lse - peak)
        den = lax.fori_loop(
            0, devices, lambda o, d: d + jnp.exp(lifted_lse(o) - peak), own_weight, unroll=small
        )
        inverse = 1.0 / den
        tables.append(own_weight * inverse)

        def slot_weight(owner, g=g, peak=peak, inverse=inverse):
            weight = jnp.exp(lifted_lse(owner) - peak) * inverse
            slot_weights[owner, pl.ds(g, 1)] = jnp.sum(weight, axis=0, keepdims=True)

        repeat(devices, slot_weight)

    low_lane = lax.broadcasted_iota(jnp.int32, (share, 2 * HD), 1) < HD

    def spread(columns, c):
        picked = [
            jnp.broadcast_to(columns[h * share : (h + 1) * share, c : c + 1], (share, 2 * HD))
            for h in range(heads)
        ]
        return jnp.concatenate(
            [jnp.where(low_lane, picked[h], picked[h + 1]) for h in range(0, heads, 2)], axis=1
        )

    def spread_slot(owner):
        columns = jnp.transpose(slot_weights[owner])
        for g in range(parts):
            scaled[owner, :, g * breadth : (g + 1) * breadth] = spread(columns, g)

    repeat(devices, spread_slot)

    own_columns = jnp.transpose(jnp.concatenate(tables, axis=0))
    for f in range(frames_here):
        for g in range(parts):
            merged[f * share : (f + 1) * share, g * breadth : (g + 1) * breadth] = (
                self_recv[g, f].astype(jnp.float32)
                * spread(own_columns, g * frames_here + f)
            ).astype(jnp.bfloat16)

    def wall_columns(n):
        return wall[:, :, n : n + 256].reshape(width, 256)

    for n in range(0, width, 256):
        base[:, n : n + 256] = jnp.dot(
            merged[...], wall_columns(n), preferred_element_type=jnp.float32
        )
    pairs_in(0)

    def scale_slot(owner):
        rows = pl.ds(owner * share, share)
        for g in range(parts):
            columns = slice(g * breadth, (g + 1) * breadth)
            slot_rows[rows, columns] = (
                pair_recv[owner, g].astype(jnp.float32) * scaled[owner, :, columns]
            ).astype(jnp.bfloat16)

    repeat(devices, scale_slot)
    for n in range(0, width, 256):
        columns = slice(n, n + 256)
        scaled[:, :, columns] = jnp.dot(
            slot_rows[...], wall_columns(n), preferred_element_type=jnp.float32
        ).reshape(devices, share, 256)
        for f in range(frames_here):

            def add(owner, state, f=f, columns=columns):
                hit = idx_recv[owner] == f
                hit = jnp.concatenate([hit] * (share // hit.shape[0]), axis=0)
                hit = jnp.concatenate([hit] * (256 // hit.shape[1]), axis=1)
                return state + jnp.where(hit, scaled[owner, :, columns], 0.0)

            state = lax.fori_loop(
                0, devices, add, base[f * share : (f + 1) * share, columns], unroll=small
            )
            out_ref[f, :, columns] = state.astype(jnp.bfloat16)

    pairs_sent()


def local(tokens, w_qkv, w_out, pair_slots):
    frames_here, length, width = tokens.shape
    breadth = w_qkv.shape[2]
    devices = lax.axis_size("frames")
    parts = lax.axis_size("heads")
    groups = lax.axis_size("groups")
    cap = pair_slots.shape[0]
    share = length // parts
    lanes = breadth // HD * share
    cuts = 2
    bf, f32 = jnp.bfloat16, jnp.float32
    vm = pl.BlockSpec(memory_space=pltpu.VMEM)
    hbm = pl.BlockSpec(memory_space=pl.ANY)
    dma = pltpu.SemaphoreType.DMA
    vmem = pltpu.VMEM
    return pl.pallas_call(
        functools.partial(kernel, devices, parts, groups, cap),
        out_shape=pltpu.VMEM((frames_here, share, width), bf),
        in_specs=[hbm] * 4,
        out_specs=vm,
        scratch_shapes=[
            pltpu.SMEM(pair_slots.shape, jnp.int32),
            pltpu.SMEM((2, devices), jnp.int32),
            vmem((frames_here, length, width), bf),
            vmem((3, width, breadth), bf),
            vmem((parts, breadth, width), bf),
        ]
        + [vmem((frames_here, length, breadth), bf)] * 3
        + [vmem((devices, frames_here, lanes), jnp.int32)] * 2
        + [
            vmem((cuts, devices - 1, share // cuts, width), bf),
            vmem((cuts, devices - 1, length // cuts, width), bf),
        ]
        + [vmem((devices, length, breadth), bf)] * 3
        + [vmem((parts, frames_here, share, breadth), bf)] * 2
        + [vmem((parts, frames_here, lanes), f32)] * 2
        + [vmem((devices, parts, share, breadth), bf)] * 2
        + [vmem((devices, parts, 1, lanes), f32)] * 2
        + [
            vmem((devices, parts, lanes), f32),
            vmem((devices, share, width), f32),
            vmem((frames_here * share, width), bf),
            vmem((frames_here * share, width), f32),
            vmem((devices * share, width), bf),
        ]
        + [dma, dma((frames_here * length // 256,)), dma((3,)), dma]
        + [dma((devices - 1,))] * 2
        + [dma((cuts, devices - 1))] * 2
        + [dma((cuts, devices - 1, 3))] * 2
        + [dma((parts - 1, 2))] * 2
        + [dma((parts - 1,))] * 2
        + [dma((devices, parts))] * 4
        + [dma((5,))] * 2,
        compiler_params=pltpu.CompilerParams(
            collective_id=0, has_side_effects=True, vmem_limit_bytes=60 * 1024 * 1024
        ),
    )(
        pair_slots,
        tokens,
        jnp.transpose(w_qkv, (1, 0, 2)),
        w_out,
    )


def solution(mesh):
    placed = (
        P(("groups", "frames"), None, None),
        P(None, None, "heads"),
        P("heads", None),
        P(("groups", "frames"), None),
    )
    return jax.shard_map(
        local,
        mesh=mesh,
        in_specs=placed,
        out_specs=P(("groups", "frames"), "heads", None),
        check_vma=False,
    )
```

```python
import functools

import jax
import jax.numpy as jnp
from jax import lax
from jax.experimental import pallas as pl
from jax.experimental.pallas import tpu as pltpu
from jax.sharding import PartitionSpec as P

HD = 64
MESH = pl.DeviceIdType.MESH


def repeat(count, body):
    if count <= 8:
        for step in range(count):
            body(step)
    else:

        def step_body(step, carry):
            body(step)
            return carry

        lax.fori_loop(0, count, step_body, 0)


def kernel(
    devices, parts, groups, cap,
    pairs_hbm, x_hbm, w_hbm, wo_hbm, out_ref,
    pairs_ref, info, x_ref, w_ref, wall, q_ref, k_ref, v_ref,
    idx_send, idx_recv, xsend, xs, qs, ks, vs,
    self_send, self_recv, self_lse, self_lse_recv,
    pair_send, pair_recv, pair_lse, pair_lse_recv,
    slot_weights, scaled, merged, base, slot_rows,
    pairs_sem, x_sem, w_sem, wo_sem, i_send, i_recv, h_send, h_recv, g_send, g_recv,
    m_send, m_recv, ml_send, ml_recv, p_send, p_recv, pl_send, pl_recv, o_send, o_recv,
):
    me = lax.axis_index("frames")
    part = lax.axis_index("heads")
    group = lax.axis_index("groups")
    frames_here, length, breadth = q_ref.shape
    width = x_ref.shape[2]
    heads = breadth // HD
    share = length // parts
    lanes = heads * share
    per = 256 // length
    chunks = frames_here // per
    half = breadth // 2
    cuts = 2
    sub = share // cuts
    here = devices - 1
    small = devices <= 8

    def peer(step):
        if devices == 4:
            low = lax.rem(me, 2)
            high = lax.div(me, 2)
            return (
                2 * high + 1 - low,
                2 * (1 - high) + low,
                3 - me,
            )[step]
        return lax.rem(me + step + 1, devices)

    def source(step):
        if devices == 4:
            return peer(step)
        return lax.rem(me + devices - step - 1, devices)

    def slot_to(step):
        return step if devices == 4 else devices - 2 - step

    def slot_of(home):
        if devices == 4:
            low = jnp.abs(lax.rem(home, 2) - lax.rem(me, 2))
            high = jnp.abs(lax.div(home, 2) - lax.div(me, 2))
            return lax.rem(low + 2 * high + 3, 4)
        return lax.rem(me - home - 1 + 2 * devices, devices)

    order = (1, 2, 0) if devices == 4 else None

    def each_peer(body, order=order):
        if devices != 4:
            repeat(devices - 1, body)
        else:
            for step in order:
                body(step)

    def head_peer(step):
        return lax.rem(part + step, parts)

    mate = part + 1 - 2 * lax.rem(part, 2)
    across = lax.rem(part + 2, parts)

    def own_rows(block):
        return pl.ds(pl.multiple_of(block * sub, sub), sub)

    barrier = pltpu.get_barrier_semaphore()

    def greet(step):
        pl.semaphore_signal(
            barrier, inc=1, device_id={"frames": peer(step)}, device_id_type=MESH
        )

    repeat(devices - 1, lambda s: greet(devices - 2 - s))
    for j in range(1, parts):
        pl.semaphore_signal(
            barrier, inc=1, device_id={"heads": head_peer(j)}, device_id_type=MESH
        )
    for j in range(1, groups):
        pl.semaphore_signal(
            barrier, inc=1, device_id={"groups": lax.rem(group + j, groups)}, device_id_type=MESH
        )

    def x_copy(i):
        rows = pl.ds(i * per, per)
        return pltpu.make_async_copy(x_hbm.at[rows], x_ref.at[rows], x_sem.at[i])

    def w_load(which):
        return pltpu.make_async_copy(w_hbm.at[which], w_ref.at[which], w_sem.at[which])

    pairs_load = pltpu.make_async_copy(pairs_hbm, pairs_ref, pairs_sem)
    pairs_load.start()
    wo_load = pltpu.make_async_copy(wo_hbm, wall.at[part], wo_sem)
    w_load(1).start()
    for i in range(chunks):
        x_copy(i).start()
    wo_load.start()
    w_load(2).start()
    w_load(0).start()

    def look(slot):
        home = me if isinstance(slot, int) and slot == here else source(slot)
        low = home * frames_here
        frame = jnp.int32(-1)
        partner = jnp.int32(0) + me
        for row in range(cap):
            a = pairs_ref[row, 0]
            b = pairs_ref[row, 1]
            hit_a = (a >= low) & (a < low + frames_here)
            hit_b = (b >= low) & (b < low + frames_here)
            frame = jnp.where(hit_a, a - low, jnp.where(hit_b, b - low, frame))
            partner = jnp.where(
                hit_a, lax.div(b, jnp.int32(frames_here)),
                jnp.where(hit_b, lax.div(a, jnp.int32(frames_here)), partner),
            )
        info[0, slot] = jnp.maximum(frame, 0)
        info[1, slot] = slot_of(partner)
        idx_send[slot] = jnp.full(idx_send.shape[1:], frame, jnp.int32)

    pairs_load.wait()
    repeat(devices - 1, look)
    look(here)
    idx_recv[here] = idx_send[here]

    def idx_copy(step):
        to = peer(step)
        return pltpu.make_async_remote_copy(
            idx_send.at[slot_to(step)], idx_recv.at[step], i_send.at[step], i_recv.at[step],
            device_id={"frames": to}, device_id_type=MESH,
        )

    def hop(step, cut):
        return pltpu.make_async_remote_copy(
            xsend.at[cut, step], xs.at[cut, step, own_rows(part)],
            h_send.at[cut, step], h_recv.at[cut, step],
            device_id={"frames": peer(step)}, device_id_type=MESH,
        )

    def g_copy(step, cut, kind):
        piece = xs.at[cut, step, own_rows(across if kind == 2 else part)]
        return pltpu.make_async_remote_copy(
            piece, piece, g_send.at[cut, step, kind], g_recv.at[cut, step, kind],
            device_id={"heads": across if kind == 1 else mate}, device_id_type=MESH,
        )

    first_half = pl.ds(pl.multiple_of(group * half, half), half)
    second_half = pl.ds(pl.multiple_of((1 - group) * half, half), half)

    def w_copy(kind):
        piece = (
            wall.at[part],
            wall.at[part, first_half],
            wall.at[across, first_half],
            wall.at[across, first_half],
            wall.at[across, second_half],
        )[kind]
        target = (
            {"heads": mate},
            {"heads": across},
            {"groups": 1 - group},
            {"heads": mate},
            {"heads": mate},
        )[kind]
        return pltpu.make_async_remote_copy(
            piece, piece, o_send.at[kind], o_recv.at[kind],
            device_id=target, device_id_type=MESH,
        )

    def m_copy(step, i):
        to = head_peer(step)
        frames = pl.ds(i * (frames_here // 2), frames_here // 2)
        return pltpu.make_async_remote_copy(
            self_send.at[to, frames], self_recv.at[part, frames],
            m_send.at[step - 1, i], m_recv.at[step - 1, i],
            device_id={"heads": to}, device_id_type=MESH,
        )

    def ml_copy(step):
        to = head_peer(step)
        return pltpu.make_async_remote_copy(
            self_lse.at[to], self_lse_recv.at[part], ml_send.at[step - 1], ml_recv.at[step - 1],
            device_id={"heads": to}, device_id_type=MESH,
        )

    def pair_copies(step, j):
        own = isinstance(step, int) and step == devices - 1
        slot = step if own else slot_to(step)
        to = head_peer(j)
        where = {"heads": to} if own else {"frames": peer(step), "heads": to}
        return (
            pltpu.make_async_remote_copy(
                pair_send.at[slot, to], pair_recv.at[step, part],
                p_send.at[step, j], p_recv.at[step, j],
                device_id=where, device_id_type=MESH,
            ),
            pltpu.make_async_remote_copy(
                pair_lse.at[slot, to], pair_lse_recv.at[step, part],
                pl_send.at[step, j], pl_recv.at[step, j],
                device_id=where, device_id_type=MESH,
            ),
        )

    pl.semaphore_wait(barrier, devices - 1 + parts - 1 + groups - 1)
    repeat(devices - 1, lambda s: idx_copy(devices - 2 - s).start())
    wo_load.wait()
    w_copy(1).start()
    w_copy(0).start()

    def project(which, target, first):
        w_load(which).wait()

        def body(i, carry):
            if first:
                x_copy(i).wait()
            rows = x_ref[pl.ds(i * per, per)].reshape(per * length, width)
            made = jnp.dot(rows, w_ref[which], preferred_element_type=jnp.float32)
            if which == 0:
                made = made * (HD ** -0.5)
            target[pl.ds(i * per, per)] = made.astype(jnp.bfloat16).reshape(per, length, breadth)
            return carry

        lax.fori_loop(0, chunks, body, 0)

    project(1, k_ref, True)

    def select(step, cut):
        asked = idx_recv[slot_to(step)]
        rows = pl.ds(pl.multiple_of(part * share + cut * sub, sub), sub)
        total = None
        for f in range(frames_here):
            unit = jnp.where(asked == f, 1.0, 0.0)
            unit = jnp.concatenate([unit, unit], axis=0).astype(jnp.bfloat16)
            unit = jnp.concatenate([unit] * (width // unit.shape[1]), axis=1)
            unit = jnp.concatenate([unit] * (sub // unit.shape[0]), axis=0)
            term = x_ref[f, rows] * unit
            total = term if total is None else total + term
        xsend[cut, step] = total

    if order is None:
        repeat(devices - 1, lambda s: idx_copy(s).wait_recv())
    for cut in range(cuts):

        def select_send(step, cut=cut):
            if cut == 0 and order is not None:
                idx_copy(step).wait_recv()
            select(step, cut)
            hop(step, cut).start()

        each_peer(select_send, (2, 0, 1))

    project(2, v_ref, False)
    project(0, q_ref, False)

    lane_head = lax.broadcasted_iota(jnp.int32, (share, breadth), 1) // HD

    def attend(blocks, key_rows, values):
        nothing = jnp.zeros((share, breadth), jnp.bfloat16)
        outs, lses = [], []
        for first in range(0, parts, 4):
            stacked = jnp.concatenate(
                [
                    jnp.where(lane_head == h, blocks[p], nothing)
                    for p in range(first, first + 4)
                    for h in range(heads)
                ],
                axis=0,
            )
            scores = lax.dot_general(
                key_rows, stacked, (((1,), (1,)), ((), ())), preferred_element_type=jnp.float32
            )
            peak = jnp.max(scores, axis=0, keepdims=True)
            lifted = jnp.exp(scores - peak)
            total = jnp.sum(lifted, axis=0, keepdims=True)
            shares = (lifted * (1.0 / total)).astype(jnp.bfloat16)
            lse = peak + jnp.log(total)
            wide = lax.dot_general(
                shares, values, (((0,), (0,)), ((), ())), preferred_element_type=jnp.float32
            )
            for p in range(4):
                rows = wide[p * lanes : (p + 1) * lanes]
                shown = rows[:share]
                for h in range(1, heads):
                    shown = jnp.where(lane_head == h, rows[h * share : (h + 1) * share], shown)
                outs.append(shown.astype(jnp.bfloat16))
                lses.append(lse[:, p * lanes : (p + 1) * lanes])
        return outs, lses

    def self_body(f, carry):
        queries = q_ref[f]
        outs, lses = attend(
            [queries[p * share : (p + 1) * share] for p in range(parts)], k_ref[f], v_ref[f]
        )
        for p in range(parts):
            self_send[p, f] = outs[p]
            self_lse[p, pl.ds(f, 1)] = lses[p]
        return carry

    part_frames = frames_here // 2
    def self_part(i):
        lax.fori_loop(i * part_frames, (i + 1) * part_frames, self_body, 0, unroll=4)

    self_part(0)

    own = info[0, here]
    ks[here] = k_ref[own]
    vs[here] = v_ref[own]
    queries = q_ref[own]
    for cut in range(cuts):
        for p in range(parts):
            low = p * share + cut * sub
            qs[here, (cut * parts + p) * sub : (cut * parts + p + 1) * sub] = queries[low : low + sub]

    piece_rows = parts * sub

    def project_piece(cut):
        rows = pl.ds(cut * piece_rows, piece_rows)

        def one(slots, count):
            taken = xs[cut, slots].reshape(count * piece_rows, width)
            for which, target in ((1, ks), (2, vs), (0, qs)):
                made = jnp.dot(taken, w_ref[which], preferred_element_type=jnp.float32)
                if which == 0:
                    made = made * (HD ** -0.5)
                target[slots, rows] = made.astype(jnp.bfloat16).reshape(count, piece_rows, breadth)

        if small:
            one(pl.ds(0, devices - 1), devices - 1)
        else:
            repeat(devices - 1, lambda step: one(pl.ds(step, 1), 1))

    def m_start(i):
        for j in (1, 2, 3):
            m_copy(j, i).start()

    for cut in range(cuts):

        def arrive(step, cut=cut):
            hop(step, cut).wait_recv()
            g_copy(step, cut, 0).start()
            g_copy(step, cut, 1).start()

        each_peer(arrive, (0, 2, 1))

    for cut in range(cuts):

        def forward(step, cut=cut):
            g_copy(step, cut, 1).wait_recv()
            g_copy(step, cut, 2).start()

        each_peer(forward, (0, 2, 1))
        if cut == 0:
            w_copy(1).wait_recv()
            w_copy(2).start()
            w_copy(3).start()
            self_part(1)
            m_start(0)
            m_start(1)

    for j in (1, 2, 3):
        ml_copy(j).start()
    self_recv[part] = self_send[part]
    self_lse_recv[part] = self_lse[part]

    for cut in range(cuts):

        def whole(step, cut=cut):
            g_copy(step, cut, 0).wait_recv()
            g_copy(step, cut, 2).wait_recv()

        each_peer(whole, (0, 2, 1))
        project_piece(cut)

    def attend_slot(slot):
        partner = info[1, slot]
        queries = qs[slot]
        blocks = [
            jnp.concatenate(
                [
                    queries[(cut * parts + p) * sub : (cut * parts + p + 1) * sub]
                    for cut in range(cuts)
                ],
                axis=0,
            )
            for p in range(parts)
        ]
        outs, lses = attend(blocks, ks[partner], vs[partner])
        for p in range(parts):
            pair_send[slot, p] = outs[p]
            pair_lse[slot, p] = lses[p]

    def slot_send(step):
        attend_slot(slot_to(step))
        for which in (1, 0):
            for j in range(parts):
                pair_copies(step, j)[which].start()

    each_peer(slot_send, (1, 2, 0))
    attend_slot(here)
    for which in (1, 0):
        for j in range(1, parts):
            pair_copies(here, j)[which].start()
    pair_recv[here, part] = pair_send[here, part]
    pair_lse_recv[here, part] = pair_lse[here, part]

    w_copy(2).wait_recv()
    w_copy(4).start()
    w_copy(0).wait_recv()
    for j in range(1, parts):
        for i in range(2):
            m_copy(j, i).wait_recv()
        ml_copy(j).wait_recv()
    w_copy(3).wait_recv()
    w_copy(4).wait_recv()

    def pairs_sent():
        def pair_sent(step):
            for j in range(parts):
                for copy in pair_copies(step, j):
                    copy.wait_send()

        repeat(devices - 1, pair_sent)
        for j in range(1, parts):
            for copy in pair_copies(here, j):
                copy.wait_send()

    repeat(devices - 1, lambda s: idx_copy(s).wait_send())

    def sent(step):
        for cut in range(cuts):
            hop(step, cut).wait_send()
            for kind in range(3):
                g_copy(step, cut, kind).wait_send()

    repeat(devices - 1, sent)
    for kind in range(5):
        w_copy(kind).wait_send()
    for j in range(1, parts):
        for i in range(2):
            m_copy(j, i).wait_send()
        ml_copy(j).wait_send()
    def pairs_in(which):
        def pair_in(step):
            for j in range(parts):
                pair_copies(step, j)[which].wait_recv()

        for j in range(1, parts):
            pair_copies(here, j)[which].wait_recv()
        repeat(devices - 1, pair_in)

    pairs_in(1)

    row_frame = lax.broadcasted_iota(jnp.int32, (frames_here, lanes), 0)
    tables = []
    for g in range(parts):
        own_lse = self_lse_recv[g]

        def lifted_lse(owner, g=g):
            row = jnp.broadcast_to(pair_lse_recv[owner, g], (frames_here, lanes))
            return jnp.where(idx_recv[owner] == row_frame, row, -jnp.inf)

        peak = lax.fori_loop(
            0, devices, lambda o, p: jnp.maximum(p, lifted_lse(o)), own_lse, unroll=small
        )
        own_weight = jnp.exp(own_lse - peak)
        den = lax.fori_loop(
            0, devices, lambda o, d: d + jnp.exp(lifted_lse(o) - peak), own_weight, unroll=small
        )
        inverse = 1.0 / den
        tables.append(own_weight * inverse)

        def slot_weight(owner, g=g, peak=peak, inverse=inverse):
            weight = jnp.exp(lifted_lse(owner) - peak) * inverse
            slot_weights[owner, pl.ds(g, 1)] = jnp.sum(weight, axis=0, keepdims=True)

        repeat(devices, slot_weight)

    low_lane = lax.broadcasted_iota(jnp.int32, (share, 2 * HD), 1) < HD

    def spread(columns, c):
        picked = [
            jnp.broadcast_to(columns[h * share : (h + 1) * share, c : c + 1], (share, 2 * HD))
            for h in range(heads)
        ]
        return jnp.concatenate(
            [jnp.where(low_lane, picked[h], picked[h + 1]) for h in range(0, heads, 2)], axis=1
        )

    def spread_slot(owner):
        columns = jnp.transpose(slot_weights[owner])
        for g in range(parts):
            scaled[owner, :, g * breadth : (g + 1) * breadth] = spread(columns, g)

    repeat(devices, spread_slot)

    own_columns = jnp.transpose(jnp.concatenate(tables, axis=0))
    for f in range(frames_here):
        for g in range(parts):
            merged[f * share : (f + 1) * share, g * breadth : (g + 1) * breadth] = (
                self_recv[g, f].astype(jnp.float32)
                * spread(own_columns, g * frames_here + f)
            ).astype(jnp.bfloat16)

    def wall_columns(n):
        return wall[:, :, n : n + 256].reshape(width, 256)

    for n in range(0, width, 256):
        base[:, n : n + 256] = jnp.dot(
            merged[...], wall_columns(n), preferred_element_type=jnp.float32
        )
    pairs_in(0)

    def scale_slot(owner):
        rows = pl.ds(owner * share, share)
        for g in range(parts):
            columns = slice(g * breadth, (g + 1) * breadth)
            slot_rows[rows, columns] = (
                pair_recv[owner, g].astype(jnp.float32) * scaled[owner, :, columns]
            ).astype(jnp.bfloat16)

    repeat(devices, scale_slot)
    for n in range(0, width, 256):
        columns = slice(n, n + 256)
        scaled[:, :, columns] = jnp.dot(
            slot_rows[...], wall_columns(n), preferred_element_type=jnp.float32
        ).reshape(devices, share, 256)
        for f in range(frames_here):

            def add(owner, state, f=f, columns=columns):
                hit = idx_recv[owner] == f
                hit = jnp.concatenate([hit] * (share // hit.shape[0]), axis=0)
                hit = jnp.concatenate([hit] * (256 // hit.shape[1]), axis=1)
                return state + jnp.where(hit, scaled[owner, :, columns], 0.0)

            state = lax.fori_loop(
                0, devices, add, base[f * share : (f + 1) * share, columns], unroll=small
            )
            out_ref[f, :, columns] = state.astype(jnp.bfloat16)

    pairs_sent()


def local(tokens, w_qkv, w_out, pair_slots):
    frames_here, length, width = tokens.shape
    breadth = w_qkv.shape[2]
    devices = lax.axis_size("frames")
    parts = lax.axis_size("heads")
    groups = lax.axis_size("groups")
    cap = pair_slots.shape[0]
    share = length // parts
    lanes = breadth // HD * share
    cuts = 2
    bf, f32 = jnp.bfloat16, jnp.float32
    vm = pl.BlockSpec(memory_space=pltpu.VMEM)
    hbm = pl.BlockSpec(memory_space=pl.ANY)
    dma = pltpu.SemaphoreType.DMA
    vmem = pltpu.VMEM
    return pl.pallas_call(
        functools.partial(kernel, devices, parts, groups, cap),
        out_shape=pltpu.VMEM((frames_here, share, width), bf),
        in_specs=[hbm] * 4,
        out_specs=vm,
        scratch_shapes=[
            pltpu.SMEM(pair_slots.shape, jnp.int32),
            pltpu.SMEM((2, devices), jnp.int32),
            vmem((frames_here, length, width), bf),
            vmem((3, width, breadth), bf),
            vmem((parts, breadth, width), bf),
        ]
        + [vmem((frames_here, length, breadth), bf)] * 3
        + [vmem((devices, frames_here, lanes), jnp.int32)] * 2
        + [
            vmem((cuts, devices - 1, share // cuts, width), bf),
            vmem((cuts, devices - 1, length // cuts, width), bf),
        ]
        + [vmem((devices, length, breadth), bf)] * 3
        + [vmem((parts, frames_here, share, breadth), bf)] * 2
        + [vmem((parts, frames_here, lanes), f32)] * 2
        + [vmem((devices, parts, share, breadth), bf)] * 2
        + [vmem((devices, parts, 1, lanes), f32)] * 2
        + [
            vmem((devices, parts, lanes), f32),
            vmem((devices, share, width), f32),
            vmem((frames_here * share, width), bf),
            vmem((frames_here * share, width), f32),
            vmem((devices * share, width), bf),
        ]
        + [dma, dma((frames_here * length // 256,)), dma((3,)), dma]
        + [dma((devices - 1,))] * 2
        + [dma((cuts, devices - 1))] * 2
        + [dma((cuts, devices - 1, 3))] * 2
        + [dma((parts - 1, 2))] * 2
        + [dma((parts - 1,))] * 2
        + [dma((devices, parts))] * 4
        + [dma((5,))] * 2,
        compiler_params=pltpu.CompilerParams(
            collective_id=0, has_side_effects=True, vmem_limit_bytes=60 * 1024 * 1024
        ),
    )(
        pair_slots,
        tokens,
        jnp.transpose(w_qkv, (1, 0, 2)),
        w_out,
    )


def solution(mesh):
    placed = (
        P(("groups", "frames"), None, None),
        P(None, None, "heads"),
        P("heads", None),
        P(("groups", "frames"), None),
    )
    return jax.shard_map(
        local,
        mesh=mesh,
        in_specs=placed,
        out_specs=P(("groups", "frames"), "heads", None),
        check_vma=False,
    )
```
